512 devices in a mesh: row: 32 (over y_lo, x, core), col: 16 (over z, y_hi).
Axes of the slice: x: 4, y: 8 (y_hi: 2, y_lo: 4; y = y_hi * 4 + y_lo), z: 8, core: 2. Of those that a mesh axis runs over, the one named last changes fastest.
Arguments:
- telemetry: int32 [65536, 64], P(('col', 'row')), may hold values from -127 to 127
- scales: int32 [65536], P(('col', 'row')), may hold values from 1 to 4
- bands: int32 [32, 32], replicated, may hold values from 256 to 4096
- noise: float32 [65536], P('row'), may hold values from 0.5 to 2
- start: bfloat16 [65536, 64], P(('col', 'row')), may hold values from -6 to 6
- target: bfloat16 [65536, 64], P('row'), may hold values from -6 to 6
Outputs:
- first: float32 [65536, 64], P('row')
- second: float32 [65536, 64], P('row')
The draws below stay inside these ranges and needn't reach their ends.
All inputs are finite; a program needn't handle non-finite values.
Results may differ from the reference program's by a relative error of at most 0.0023.
Values may be sent and summed in bfloat16 or wider, within the bound.
A program may use at most 128 MiB of HBM per device.

```python
import math
import jax
import jax.numpy as jnp
from jax import lax

SUBAP = 2048
FRAMES = 64
PANEL = 64
M = 65536
SENSORS = 32


def with_ends(entries, stream_key, low, top_value):
    dims = entries.shape
    index_at = [jax.random.randint(jax.random.fold_in(stream_key, axis), (), 0, dims[axis]) for axis in range(len(dims))]
    entries = entries.at[tuple(index_at)].set(low)
    longest = dims.index(max(dims))
    index_at[longest] = (index_at[longest] + 1) % dims[longest]
    return entries.at[tuple(index_at)].set(top_value)


def block_scale(own_key, dims, pieces, smallest, high):
    factor_of, own = 1.0, jax.random.fold_in(own_key, 6)
    for position, parts in pieces:
        draws = jnp.exp(jax.random.uniform(jax.random.fold_in(own, position), (parts,), jnp.float32, smallest / len(pieces), high / len(pieces)))
        factor_of = factor_of * jnp.repeat(draws, dims[position] // parts).reshape([-1 if axis == position else 1 for axis in range(len(dims))])
    return factor_of


def normal_values(rng, extent, spread, bound, shards=(), kind=jnp.bfloat16):
    array = spread * jax.random.normal(rng, extent, jnp.float32)
    if shards:
        array = array * block_scale(rng, extent, shards, -0.22, 0.18)
    return jnp.clip(array, -bound, bound).astype(kind)


def setup_inputs(seed: int = 0) -> dict:
    splits = jax.random.split(jax.random.key(seed), 7)
    return {
        "telemetry": with_ends(jax.random.randint(splits[0], (M, FRAMES), -127, 128), jax.random.fold_in(splits[0], 1), -127, 127).astype(jnp.int32),
        "scales": with_ends(jax.random.randint(splits[1], (M,), 1, 5), jax.random.fold_in(splits[1], 1), 1, 4).astype(jnp.int32),
        "bands": with_ends(jax.random.randint(splits[2], (SENSORS, SENSORS), SUBAP // 8, 2 * SUBAP + 1), jax.random.fold_in(splits[2], 1), SUBAP // 8, 2 * SUBAP).astype(jnp.int32),
        "noise": jnp.clip(jnp.exp(math.log(2.0) - 1.3862944 * jax.random.uniform(splits[3], (M,), jnp.float32) ** block_scale(splits[3], (M,), ((0, 32),), -0.2, 0.2)), 0.5, 2.0),
        "start": normal_values(splits[4], (M, PANEL), 1.0, 6.0, ((0, 512),)),
        "target": normal_values(splits[5], (M, PANEL), 1.0, 6.0, ((0, 32),)),
    }


damping = 0.4


def reference(telemetry, scales, bands, noise, start, target):
    norm_count = jnp.float32(M // 4)
    slopes = (telemetry.astype(jnp.float32) * scales.astype(jnp.float32)[:, None] / 128.0).astype(jnp.bfloat16)
    slope_f = slopes.astype(jnp.float32)
    weight = damping / (jnp.sum(slope_f * slope_f, axis=1) / norm_count + noise)
    count = bands.shape[0]
    index = jnp.arange(count, dtype=jnp.int32)
    sym = jnp.where(index[:, None] <= index[None, :], bands, bands.T).astype(jnp.float32)
    cols_all = jnp.arange(M, dtype=jnp.int32)
    col_pos = (cols_all % SUBAP).astype(jnp.float32)

    def apply(panel):
        def one(block_id):
            first_row = (block_id * SUBAP).astype(jnp.int32)
            rows = lax.dynamic_slice_in_dim(slope_f, first_row, SUBAP, 0)
            raw = jnp.dot(rows, slope_f.T, precision=lax.Precision.HIGHEST) / norm_count
            row_ids = first_row + jnp.arange(SUBAP, dtype=jnp.int32)
            band = sym[block_id][cols_all // SUBAP]
            dist = jnp.abs((row_ids % SUBAP).astype(jnp.float32)[:, None] - col_pos[None, :])
            taper = jnp.maximum(0.0, 1.0 - dist / band[None, :])
            row_noise = lax.dynamic_slice_in_dim(noise, first_row, SUBAP, 0)
            diag = jnp.where(row_ids[:, None] == cols_all[None, :], row_noise[:, None], jnp.float32(0.0))
            entry = (taper * raw + diag).astype(jnp.bfloat16)
            return jnp.dot(entry, panel, preferred_element_type=jnp.float32)

        out = lax.map(one, jnp.arange(M // SUBAP, dtype=jnp.int32))
        return out.reshape(M, panel.shape[1])

    target_f = target.astype(jnp.float32)
    product0 = apply(start)
    first = start.astype(jnp.float32) + weight[:, None] * (target_f - product0)
    product1 = apply(first.astype(jnp.bfloat16))
    second = first + weight[:, None] * (target_f - product1)
    return first, second
```

```python
import jax
import jax.numpy as jnp
from jax import lax
from jax.experimental import pallas as pl
from jax.experimental.pallas import tpu as pltpu
from jax.sharding import PartitionSpec as P

NZ, NH, NL, NX, NU = 8, 2, 4, 4, 2
NY = NH * NL
ROWS = 128
HALF = ROWS // 2
SUBAP = 2048
SHARDS = NY * NX * NU
PIECES = NZ
TILE = NU * ROWS
TILES = SHARDS // NU
TILES_SENSOR = SUBAP // TILE
SLOTS = 16
CHUNK = 4
MESH = pl.DeviceIdType.MESH
damping = 0.4
f32, bf16 = jnp.float32, jnp.bfloat16


def low_lanes(shape):
    return lax.broadcasted_iota(jnp.int32, shape, 1) < HALF


def swap(v):
    return pltpu.roll(v, HALF, 1)


def kernel(
    joined, invb, target, noise, out1, out2,
    colb, rowp, srow, scol, xcol, cov, dist, acc, bsend, brecv, dsend, drecv,
    tgt, noi, low1, low2, cbuf, ebuf1, ebuf2,
    send_a, recv_a, send_r, recv_r, send_t, recv_t, send_n, recv_n, send_b, recv_b,
    send_c, recv_c, send_d, recv_d, send_e, recv_e, send_f, recv_f,
):
    row, col = lax.axis_index("row"), lax.axis_index("col")
    z, h = col // NH, col % NH
    l, x, u = row // (NX * NU), row // NU % NX, row % NU
    y = h * NL + l

    def rowid(yy, xx, uu):
        return yy % NL * (NX * NU) + xx * NU + uu

    def colid(zz, yy):
        return zz * NH + yy // NL

    def at(zz, yy, xx, uu):
        return rowid(yy, xx, uu), colid(zz, yy)

    def shard(yy, xx, uu):
        return (yy * NX + xx) * NU + uu

    def remote(src, dst, ssem, rsem, dev):
        return pltpu.make_async_remote_copy(
            src_ref=src, dst_ref=dst, send_sem=ssem, recv_sem=rsem, device_id=dev, device_id_type=MESH
        )

    def put_maybe_self(src, dst, ssem, rsem, dev):
        mine = (dev[0] == row) & (dev[1] == col)

        @pl.when(mine)
        def _():
            pltpu.make_async_copy(src, dst, rsem).start()

        @pl.when(jnp.logical_not(mine))
        def _():
            remote(src, dst, ssem, rsem, dev).start()

    me = shard(y, x, u)
    here = (row, col)
    xl, xr, xo = (x + NX - 1) % NX, (x + 1) % NX, (x + 2) % NX
    order = [0] + [d for k in range(1, NY // 2) for d in (k, -k)] + [NY // 2]
    ys = [(y + d + NY) % NY for d in order]
    zs = [(z + d) % NZ for d in range(1, NZ)]

    barrier = pltpu.get_barrier_semaphore()
    near = [at(zz, y, x, u) for zz in zs] + [at(z, yy, x, u) for yy in ys[1:]]
    near += [at(z, y, xl, u), at(z, y, xr, u), at(z, y, x, 1 - u)]
    for dev in near:
        pl.semaphore_signal(barrier, inc=1, device_id=dev, device_id_type=MESH)
    pl.semaphore_wait(barrier, len(near))

    def plane_gather(src, buf, ssem, rsem):
        count = [0]
        sent = []

        def send(s_src, s, dev, cond=None):
            k = count[0]
            count[0] += 1
            copy = remote(s_src, buf.at[s], ssem.at[k], rsem.at[s], dev)
            sent.append((copy, cond))
            if cond is None:
                copy.start()
            else:
                pl.when(cond)(copy.start)

        def wait(s):
            remote(src, buf.at[s], ssem.at[0], rsem.at[s], here).wait_recv()

        for yy in ys[1:]:
            send(src, me, at(z, yy, x, u))
        for i, yy in enumerate(ys):
            s = shard(yy, x, u)
            if i:
                wait(s)
            s_src = buf.at[s] if i else src
            for dev in (at(z, y, xl, u), at(z, y, xr, u), at(z, y, x, 1 - u)):
                send(s_src, s, dev)
        for yy in ys:
            even = yy % 2 == 0
            sl, sr = shard(yy, xl, u), shard(yy, xr, u)
            wait(sl)
            send(buf.at[sl], sl, at(z, y, xr, u), even)
            send(buf.at[sl], sl, at(z, y, x, 1 - u))
            wait(sr)
            send(buf.at[sr], sr, at(z, y, xl, u), jnp.logical_not(even))
            send(buf.at[sr], sr, at(z, y, x, 1 - u))
        for yy in ys:
            s = shard(yy, xo, u)
            wait(s)
            send(buf.at[s], s, at(z, y, x, 1 - u))
        for yy in ys:
            for xx in range(NX):
                wait(shard(yy, xx, 1 - u))

        def drain():
            for copy, cond in sent:
                if cond is None:
                    copy.wait_send()
                else:
                    pl.when(cond)(copy.wait_send)

        return drain

    mine_s = joined.at[pl.ds(0, HALF)]
    for k, zz in enumerate(zs):
        remote(mine_s, rowp.at[z], send_r.at[k], recv_r.at[z], at(zz, y, x, u)).start()
    drain_a = plane_gather(joined, colb, send_a, recv_a)

    source = (l == z // 2) & (x // 2 == z % 2)
    owner_dev = []
    for xx in range(NX):
        for uu in range(NU):
            slot = h * (NX * NU) + xx * NU + uu
            dev = ((2 * u + h) * (NX * NU) + xx * NU + uu, z * NH + x % NH)
            owner_dev.append((slot, dev))

    @pl.when(source)
    def _():
        for k, (slot, dev) in enumerate(owner_dev):
            off = pl.multiple_of(slot * ROWS, ROWS)
            put_maybe_self(target.at[pl.ds(off, ROWS)], tgt, send_t.at[k], recv_t, dev)
            put_maybe_self(noise.at[slot], noi, send_n.at[k], recv_n, dev)

    colb[me] = joined[...]

    def unpack(s, carry):
        base = pl.multiple_of(s * ROWS, ROWS)
        sp = colb[s, :HALF, :]
        xp = colb[s, HALF:, :]
        scol[pl.ds(base, HALF), :] = sp
        scol[pl.ds(pl.multiple_of(base + HALF, HALF), HALF), :] = swap(sp.astype(f32)).astype(bf16)
        xcol[pl.ds(base, HALF), :] = xp
        xcol[pl.ds(pl.multiple_of(base + HALF, HALF), HALF), :] = swap(xp.astype(f32)).astype(bf16)
        return carry

    lax.fori_loop(0, SHARDS, unpack, 0)
    for zz in zs:
        remote(mine_s, rowp.at[zz], send_r.at[0], recv_r.at[zz], here).wait_recv()
    rowp[z] = joined[:HALF, :]
    keep = low_lanes((HALF, ROWS))
    for j in range(PIECES):
        v = rowp[j].astype(f32) * (1.0 / 16384.0)
        srow[pl.ds(j * ROWS, HALF), :] = jnp.where(keep, v, 0.0).astype(bf16)
        srow[pl.ds(j * ROWS + HALF, HALF), :] = jnp.where(keep, swap(v), 0.0).astype(bf16)

    p0 = (l % 2 * (NX * NU) + x * NU + u) * ROWS
    base_d = (
        p0 + lax.broadcasted_iota(jnp.int32, (ROWS, TILE), 0) - lax.broadcasted_iota(jnp.int32, (ROWS, TILE), 1)
    )
    for t in range(TILES_SENSOR):
        dist[t] = jnp.abs(base_d - t * TILE).astype(f32)

    contract_last = (((1,), (1,)), ((), ()))

    def pack_piece(j):
        r = pl.multiple_of(j * ROWS, ROWS)
        lo = acc[pl.ds(r, HALF), :]
        hi = acc[pl.ds(pl.multiple_of(r + HALF, HALF), HALF), :]
        return jnp.where(keep, lo, swap(hi))

    def send_piece(j, sbuf, rbuf, ssem, rsem):
        sbuf[j] = pack_piece(j)

        @pl.when(j != z)
        def _():
            remote(sbuf.at[j], rbuf.at[z], ssem.at[j], rsem.at[z], at(j, y, x, u)).start()

    for c in range(PIECES // CHUNK):
        span = pl.ds(c * CHUNK * ROWS, CHUNK * ROWS)
        acc[span, :] = jnp.zeros((CHUNK * ROWS, ROWS), f32)

        def build(t, carry):
            cols = pl.ds(pl.multiple_of(t * TILE, TILE), TILE)
            raw = lax.dot_general(srow[span, :], scol[cols, :], contract_last, preferred_element_type=f32)
            d = dist[t % TILES_SENSOR]
            parts = []
            for i in range(CHUNK):
                j = c * CHUNK + i
                inv = invb[NL * j + y // 2, NL * z + t // TILES_SENSOR]
                taper = jnp.maximum(0.0, 1.0 - d * inv)
                parts.append((taper * raw[i * ROWS : (i + 1) * ROWS, :]).astype(bf16))
            entry = jnp.concatenate(parts, axis=0)
            cov[t, span, :] = entry
            acc[span, :] += jnp.dot(entry, xcol[cols, :], preferred_element_type=f32)
            return carry

        lax.fori_loop(0, TILES, build, 0)
        for i in range(CHUNK):
            send_piece(c * CHUNK + i, bsend, brecv, send_b, recv_b)

    def collected(sbuf, rbuf, rsem):
        total = sbuf[z]
        for zz in zs:
            remote(sbuf.at[0], rbuf.at[zz], send_b.at[0], rsem.at[zz], here).wait_recv()
            total = total + rbuf[zz]
        return total

    remote(target.at[pl.ds(0, ROWS)], tgt, send_t.at[0], recv_t, here).wait_recv()
    remote(noise.at[0], noi, send_n.at[0], recv_n, here).wait_recv()
    s_own = joined[:HALF, :].astype(f32)
    x_own = joined[HALF:, :].astype(f32)
    sq = s_own * s_own
    raw_lo = jnp.sum(jnp.where(keep, sq, 0.0), axis=1, keepdims=True)
    raw_hi = jnp.sum(jnp.where(keep, 0.0, sq), axis=1, keepdims=True)
    raw_own = jnp.where(keep, raw_lo, raw_hi) * (1.0 / 16384.0)
    noise_t = jnp.transpose(jnp.broadcast_to(noi[0:1, :], (ROWS, ROWS)))
    noise_own = jnp.where(keep, noise_t[:HALF], noise_t[HALF:])
    tgt_f = tgt[...].astype(f32)
    tgt_own = jnp.concatenate([tgt_f[:HALF], tgt_f[HALF:]], axis=1)
    diag = raw_own + noise_own
    weight = damping / diag
    extra = diag.astype(bf16).astype(f32) - raw_own.astype(bf16).astype(f32)

    first = x_own + weight * (tgt_own - (collected(bsend, brecv, recv_b) + extra * x_own))
    low1[...] = first.astype(bf16)

    out_row = (z // 2) * (NX * NU) + (z % 2 * 2 + h) * NU + l // 2
    slot_me = l % 2 * (NX * NU) + x * NU + u
    outs = [(zz * NH + hh) for zz in range(NZ) for hh in range(NH)]

    def spread(src, buf, ssem, rsem):
        for k, cc in enumerate(outs):
            put_maybe_self(src, buf.at[slot_me], ssem.at[k], rsem.at[slot_me], (out_row, cc))

    def spread_sent(src, buf, ssem, rsem):
        for k, cc in enumerate(outs):
            @pl.when(jnp.logical_not((out_row == row) & (cc == col)))
            def _():
                remote(src, buf.at[slot_me], ssem.at[k], rsem.at[slot_me], (out_row, cc)).wait_send()

    def unpack_out(src, buf, rsem, out):
        for s in range(SLOTS):
            remote(src, buf.at[s], send_e.at[0], rsem.at[s], here).wait_recv()
            v = buf[s].astype(f32)
            out[pl.ds(s * ROWS, HALF), :] = v[:, :HALF].astype(bf16)
            out[pl.ds(s * ROWS + HALF, HALF), :] = swap(v)[:, :HALF].astype(bf16)

    drain_c = plane_gather(low1, cbuf, send_c, recv_c)
    spread(low1, ebuf1, send_e, recv_e)
    cbuf[me] = low1[...]

    def unpack_first(s, carry):
        base = pl.multiple_of(s * ROWS, ROWS)
        xp = cbuf[s]
        xcol[pl.ds(base, HALF), :] = xp
        xcol[pl.ds(pl.multiple_of(base + HALF, HALF), HALF), :] = swap(xp.astype(f32)).astype(bf16)
        return carry

    lax.fori_loop(0, SHARDS, unpack_first, 0)

    for c in range(PIECES // CHUNK):
        span = pl.ds(c * CHUNK * ROWS, CHUNK * ROWS)
        acc[span, :] = jnp.zeros((CHUNK * ROWS, ROWS), f32)

        def multiply(t, carry):
            cols = pl.ds(pl.multiple_of(t * TILE, TILE), TILE)
            acc[span, :] += jnp.dot(cov[t, span, :], xcol[cols, :], preferred_element_type=f32)
            return carry

        lax.fori_loop(0, TILES, multiply, 0)
        for i in range(CHUNK):
            send_piece(c * CHUNK + i, dsend, drecv, send_d, recv_d)

    product1 = collected(dsend, drecv, recv_d) + extra * first.astype(bf16).astype(f32)
    low2[...] = (first + weight * (tgt_own - product1)).astype(bf16)
    spread(low2, ebuf2, send_f, recv_f)
    unpack_out(low1, ebuf1, recv_e, out1)
    unpack_out(low2, ebuf2, recv_f, out2)

    drain_a()
    drain_c()
    for k, zz in enumerate(zs):
        remote(mine_s, rowp.at[z], send_r.at[k], recv_r.at[z], at(zz, y, x, u)).wait_send()

    @pl.when(source)
    def _():
        for k, (slot, dev) in enumerate(owner_dev):
            off = pl.multiple_of(slot * ROWS, ROWS)

            @pl.when(jnp.logical_not((dev[0] == row) & (dev[1] == col)))
            def _():
                remote(target.at[pl.ds(off, ROWS)], tgt, send_t.at[k], recv_t, dev).wait_send()
                remote(noise.at[slot], noi, send_n.at[k], recv_n, dev).wait_send()

    for j in range(PIECES):
        @pl.when(j != z)
        def _():
            remote(bsend.at[j], brecv.at[z], send_b.at[j], recv_b.at[z], at(j, y, x, u)).wait_send()
            remote(dsend.at[j], drecv.at[z], send_d.at[j], recv_d.at[z], at(j, y, x, u)).wait_send()

    spread_sent(low1, ebuf1, send_e, recv_e)
    spread_sent(low2, ebuf2, send_f, recv_f)


def pack(a):
    return jnp.concatenate([a[:HALF], a[HALF:]], axis=1)


def on_device(telemetry, scales, bands, noise, start, target):
    slopes = (telemetry.astype(f32) * scales.astype(f32)[:, None] / 128.0).astype(bf16)
    joined = jnp.concatenate([pack(slopes), pack(start)], axis=0)
    index = jnp.arange(bands.shape[0], dtype=jnp.int32)
    sym = jnp.where(index[:, None] <= index[None, :], bands, bands.T).astype(f32)
    invb = 1.0 / sym
    noise = jnp.broadcast_to(noise.reshape(SLOTS, 1, ROWS), (SLOTS, 8, ROWS))
    vmem = pl.BlockSpec(memory_space=pltpu.VMEM)
    dma, gathers = pltpu.SemaphoreType.DMA, SHARDS + 8
    out = jax.ShapeDtypeStruct(target.shape, bf16)
    packed = (HALF, ROWS)
    first, second = pl.pallas_call(
        kernel,
        out_shape=(out, out),
        in_specs=[vmem, pl.BlockSpec(memory_space=pltpu.SMEM), vmem, vmem],
        out_specs=(vmem, vmem),
        scratch_shapes=[
            pltpu.VMEM((SHARDS, ROWS, ROWS), bf16),
            pltpu.VMEM((PIECES, *packed), bf16),
            pltpu.VMEM((PIECES * ROWS, ROWS), bf16),
            pltpu.VMEM((SHARDS * ROWS, ROWS), bf16),
            pltpu.VMEM((SHARDS * ROWS, ROWS), bf16),
            pltpu.VMEM((TILES, PIECES * ROWS, TILE), bf16),
            pltpu.VMEM((TILES_SENSOR, ROWS, TILE), f32),
            pltpu.VMEM((PIECES * ROWS, ROWS), f32),
            pltpu.VMEM((PIECES, *packed), f32),
            pltpu.VMEM((PIECES, *packed), f32),
            pltpu.VMEM((PIECES, *packed), f32),
            pltpu.VMEM((PIECES, *packed), f32),
            pltpu.VMEM((ROWS, HALF), bf16),
            pltpu.VMEM((8, ROWS), f32),
            pltpu.VMEM(packed, bf16),
            pltpu.VMEM(packed, bf16),
            pltpu.VMEM((SHARDS, *packed), bf16),
            pltpu.VMEM((SLOTS, *packed), bf16),
            pltpu.VMEM((SLOTS, *packed), bf16),
            dma((gathers + 8,)), dma((SHARDS,)),
            dma((NZ,)), dma((NZ,)),
            dma((8,)), dma,
            dma((8,)), dma,
            dma((NZ,)), dma((NZ,)),
            dma((gathers + 8,)), dma((SHARDS,)),
            dma((NZ,)), dma((NZ,)),
            dma((SLOTS,)), dma((SLOTS,)),
            dma((SLOTS,)), dma((SLOTS,)),
        ],
        compiler_params=pltpu.CompilerParams(
            collective_id=0, has_side_effects=True, vmem_limit_bytes=60 * 2**20
        ),
    )(joined, invb, target, noise)
    return first.astype(f32), second.astype(f32)


def solution(mesh):
    placed = (P(("col", "row"), None), P(("col", "row")), P(), P("row"), P(("col", "row"), None), P("row", None))
    return jax.shard_map(
        on_device,
        mesh=mesh,
        in_specs=placed,
        out_specs=(P("row", None), P("row", None)),
        check_vma=False,
    )
```

```python
import jax
import jax.numpy as jnp
from jax import lax
from jax.experimental import pallas as pl
from jax.experimental.pallas import tpu as pltpu
from jax.sharding import PartitionSpec as P

NZ, NH, NL, NX, NU = 8, 2, 4, 4, 2
NY = NH * NL
ROWS = 128
HALF = ROWS // 2
SUBAP = 2048
SHARDS = NY * NX * NU
PIECES = NZ
TILE = NU * ROWS
TILES = SHARDS // NU
TILES_SENSOR = SUBAP // TILE
SLOTS = 16
CHUNK = 4
MESH = pl.DeviceIdType.MESH
damping = 0.4
f32, bf16 = jnp.float32, jnp.bfloat16


def kernel(
    telemetry, scales, bands, noise, start, target, out1, out2,
    joined, colb, rowp, srow, inv, cov, dist, acc, bsend, brecv, dsend, drecv,
    tgt, noises, noi, low1, low2, cbuf, ebuf1, ebuf2,
    send_a, recv_a, send_r, recv_r, send_t, recv_t, send_n, recv_n, send_b, recv_b,
    send_c, recv_c, send_d, recv_d, send_e, recv_e, send_f, recv_f,
):
    row, col = lax.axis_index("row"), lax.axis_index("col")
    z, h = col // NH, col % NH
    l, x, u = row // (NX * NU), row // NU % NX, row % NU
    y = h * NL + l

    def rowid(yy, xx, uu):
        return yy % NL * (NX * NU) + xx * NU + uu

    def colid(zz, yy):
        return zz * NH + yy // NL

    def at(zz, yy, xx, uu):
        return rowid(yy, xx, uu), colid(zz, yy)

    def shard(yy, xx, uu):
        return (yy * NX + xx) * NU + uu

    def remote(src, dst, ssem, rsem, dev):
        return pltpu.make_async_remote_copy(
            src_ref=src, dst_ref=dst, send_sem=ssem, recv_sem=rsem, device_id=dev, device_id_type=MESH
        )

    def put_maybe_self(src, dst, ssem, rsem, dev):
        mine = (dev[0] == row) & (dev[1] == col)

        @pl.when(mine)
        def _():
            pltpu.make_async_copy(src, dst, rsem).start()

        @pl.when(jnp.logical_not(mine))
        def _():
            remote(src, dst, ssem, rsem, dev).start()

    me = shard(y, x, u)
    here = (row, col)
    xl, xr, xo = (x + NX - 1) % NX, (x + 1) % NX, (x + 2) % NX
    order = [0] + [d for k in range(1, NY // 2) for d in (k, -k)] + [NY // 2]
    ys = [(y + d + NY) % NY for d in order]
    zs = [(z + d) % NZ for d in range(1, NZ)]

    barrier = pltpu.get_barrier_semaphore()
    near = [at(zz, y, x, u) for zz in zs] + [at(z, yy, x, u) for yy in ys[1:]]
    near += [at(z, y, xl, u), at(z, y, xr, u), at(z, y, x, 1 - u)]
    for dev in near:
        pl.semaphore_signal(barrier, inc=1, device_id=dev, device_id_type=MESH)

    slopes = telemetry[...].astype(f32) * scales[...].astype(f32) * (1.0 / 128.0)
    joined[:HALF, :] = slopes.astype(bf16)
    joined[HALF:, :] = start[...]
    for s in range(SLOTS):
        noises[s] = jnp.broadcast_to(noise[s : s + 1, :], (8, ROWS))
    pl.semaphore_wait(barrier, len(near))

    def plane_gather(src, buf, ssem, rsem):
        count = [0]
        sent = []

        def send(s_src, s, dev, cond=None):
            k = count[0]
            count[0] += 1
            copy = remote(s_src, buf.at[s], ssem.at[k], rsem.at[s], dev)
            sent.append((copy, cond))
            if cond is None:
                copy.start()
            else:
                pl.when(cond)(copy.start)

        def wait(s):
            remote(src, buf.at[s], ssem.at[0], rsem.at[s], here).wait_recv()

        for yy in ys[1:]:
            send(src, me, at(z, yy, x, u))
        for i, yy in enumerate(ys):
            s = shard(yy, x, u)
            if i:
                wait(s)
            s_src = buf.at[s] if i else src
            for dev in (at(z, y, xl, u), at(z, y, xr, u), at(z, y, x, 1 - u)):
                send(s_src, s, dev)
        for yy in ys:
            even = yy % 2 == 0
            sl, sr = shard(yy, xl, u), shard(yy, xr, u)
            wait(sl)
            send(buf.at[sl], sl, at(z, y, xr, u), even)
            send(buf.at[sl], sl, at(z, y, x, 1 - u))
            wait(sr)
            send(buf.at[sr], sr, at(z, y, xl, u), jnp.logical_not(even))
            send(buf.at[sr], sr, at(z, y, x, 1 - u))
        for yy in ys:
            s = shard(yy, xo, u)
            wait(s)
            send(buf.at[s], s, at(z, y, x, 1 - u))
        for yy in ys:
            for xx in range(NX):
                wait(shard(yy, xx, 1 - u))

        def drain():
            for copy, cond in sent:
                if cond is None:
                    copy.wait_send()
                else:
                    pl.when(cond)(copy.wait_send)

        return drain

    mine_s = joined.at[pl.ds(0, HALF)]
    for k, zz in enumerate(zs):
        remote(mine_s, rowp.at[z], send_r.at[k], recv_r.at[z], at(zz, y, x, u)).start()
    drain_a = plane_gather(joined, colb, send_a, recv_a)

    def target_part(slot):
        return target.at[:, pl.ds(pl.multiple_of(slot * ROWS, ROWS), ROWS)]

    source = (l == z // 2) & (x // 2 == z % 2)
    owner_dev = []
    for xx in range(NX):
        for uu in range(NU):
            slot = h * (NX * NU) + xx * NU + uu
            dev = ((2 * u + h) * (NX * NU) + xx * NU + uu, z * NH + x % NH)
            owner_dev.append((slot, dev))

    @pl.when(source)
    def _():
        for k, (slot, dev) in enumerate(owner_dev):
            put_maybe_self(target_part(slot), tgt, send_t.at[k], recv_t, dev)
            put_maybe_self(noises.at[slot], noi, send_n.at[k], recv_n, dev)

    for j in range(PIECES):
        for k in range(NL):
            a, b = NL * j + y // 2, NL * z + k
            band = bands[jnp.minimum(a, b), jnp.maximum(a, b)].astype(f32)
            inv[j * NL + k] = 1.0 / jnp.full((1, TILE), band, f32)

    p0 = (l % 2 * (NX * NU) + x * NU + u) * ROWS
    base_d = (
        p0 + lax.broadcasted_iota(jnp.int32, (ROWS, TILE), 0) - lax.broadcasted_iota(jnp.int32, (ROWS, TILE), 1)
    )
    for t in range(TILES_SENSOR):
        dist[t] = jnp.abs(base_d - t * TILE).astype(f32)

    colb[me] = joined[...]
    for zz in zs:
        remote(mine_s, rowp.at[zz], send_r.at[0], recv_r.at[zz], here).wait_recv()
    rowp[z] = joined[:HALF, :]
    for j in range(PIECES):
        v = rowp[j].astype(f32) * (1.0 / 16384.0)
        srow[pl.ds(j * ROWS, ROWS), :] = jnp.transpose(v).astype(bf16)

    contract_last = (((1,), (1,)), ((), ()))

    def pack_piece(j):
        return jnp.transpose(acc[pl.ds(pl.multiple_of(j * ROWS, ROWS), ROWS), :])

    def pair(ref, t, part):
        return jnp.concatenate([ref[NU * t + i, part, :] for i in range(NU)], axis=1)

    slope_rows, panel_rows = slice(0, HALF), slice(HALF, ROWS)

    def send_piece(j, sbuf, rbuf, ssem, rsem):
        sbuf[j] = pack_piece(j)

        @pl.when(j != z)
        def _():
            remote(sbuf.at[j], rbuf.at[z], ssem.at[j], rsem.at[z], at(j, y, x, u)).start()

    for c in range(PIECES // CHUNK):
        span = pl.ds(c * CHUNK * ROWS, CHUNK * ROWS)
        acc[span, :] = jnp.zeros((CHUNK * ROWS, HALF), f32)

        def build(t, carry):
            raw = jnp.dot(srow[span, :], pair(colb, t, slope_rows), preferred_element_type=f32)
            d = dist[t % TILES_SENSOR]
            parts = []
            for i in range(CHUNK):
                j = c * CHUNK + i
                taper = jnp.maximum(0.0, 1.0 - d * inv[j * NL + t // TILES_SENSOR])
                parts.append((taper * raw[i * ROWS : (i + 1) * ROWS, :]).astype(bf16))
            entry = jnp.concatenate(parts, axis=0)
            cov[t, span, :] = entry
            acc[span, :] += lax.dot_general(
                entry, pair(colb, t, panel_rows), contract_last, preferred_element_type=f32
            )
            return carry

        lax.fori_loop(0, TILES, build, 0)
        for i in range(CHUNK):
            send_piece(c * CHUNK + i, bsend, brecv, send_b, recv_b)

    def collected(sbuf, rbuf, rsem):
        total = sbuf[z]
        for zz in zs:
            remote(sbuf.at[0], rbuf.at[zz], send_b.at[0], rsem.at[zz], here).wait_recv()
            total = total + rbuf[zz]
        return total

    remote(target_part(0), tgt, send_t.at[0], recv_t, here).wait_recv()
    remote(noises.at[0], noi, send_n.at[0], recv_n, here).wait_recv()
    s_own = joined[:HALF, :].astype(f32)
    x_own = joined[HALF:, :].astype(f32)
    raw_own = jnp.sum(s_own * s_own, axis=0, keepdims=True) * (1.0 / 16384.0)
    diag = raw_own + noi[0:1, :]
    weight = damping / diag
    extra = diag.astype(bf16).astype(f32) - raw_own.astype(bf16).astype(f32)
    tgt_own = tgt[...].astype(f32)

    first = x_own + weight * (tgt_own - (collected(bsend, brecv, recv_b) + extra * x_own))
    low1[...] = first.astype(bf16)

    out_row = (z // 2) * (NX * NU) + (z % 2 * 2 + h) * NU + l // 2
    slot_me = l % 2 * (NX * NU) + x * NU + u
    outs = [(zz * NH + hh) for zz in range(NZ) for hh in range(NH)]

    def spread(src, buf, ssem, rsem):
        for k, cc in enumerate(outs):
            put_maybe_self(src, buf.at[slot_me], ssem.at[k], rsem.at[slot_me], (out_row, cc))

    def spread_sent(src, buf, ssem, rsem):
        for k, cc in enumerate(outs):
            @pl.when(jnp.logical_not((out_row == row) & (cc == col)))
            def _():
                remote(src, buf.at[slot_me], ssem.at[k], rsem.at[slot_me], (out_row, cc)).wait_send()

    def unpack_out(src, buf, rsem, out):
        for s in range(SLOTS):
            remote(src, buf.at[s], send_e.at[0], rsem.at[s], here).wait_recv()
            out[:, pl.ds(s * ROWS, ROWS)] = buf[s]

    drain_c = plane_gather(low1, cbuf, send_c, recv_c)
    spread(low1, ebuf1, send_e, recv_e)
    cbuf[me] = low1[...]

    for c in range(PIECES // CHUNK):
        span = pl.ds(c * CHUNK * ROWS, CHUNK * ROWS)
        acc[span, :] = jnp.zeros((CHUNK * ROWS, HALF), f32)

        def multiply(t, carry):
            acc[span, :] += lax.dot_general(
                cov[t, span, :], pair(cbuf, t, slice(None)), contract_last, preferred_element_type=f32
            )
            return carry

        lax.fori_loop(0, TILES, multiply, 0)
        for i in range(CHUNK):
            send_piece(c * CHUNK + i, dsend, drecv, send_d, recv_d)

    product1 = collected(dsend, drecv, recv_d) + extra * first.astype(bf16).astype(f32)
    low2[...] = (first + weight * (tgt_own - product1)).astype(bf16)
    spread(low2, ebuf2, send_f, recv_f)
    unpack_out(low1, ebuf1, recv_e, out1)
    unpack_out(low2, ebuf2, recv_f, out2)

    drain_a()
    drain_c()
    for k, zz in enumerate(zs):
        remote(mine_s, rowp.at[z], send_r.at[k], recv_r.at[z], at(zz, y, x, u)).wait_send()

    @pl.when(source)
    def _():
        for k, (slot, dev) in enumerate(owner_dev):
            @pl.when(jnp.logical_not((dev[0] == row) & (dev[1] == col)))
            def _():
                remote(target_part(slot), tgt, send_t.at[k], recv_t, dev).wait_send()
                remote(noises.at[slot], noi, send_n.at[k], recv_n, dev).wait_send()

    for j in range(PIECES):
        @pl.when(j != z)
        def _():
            remote(bsend.at[j], brecv.at[z], send_b.at[j], recv_b.at[z], at(j, y, x, u)).wait_send()
            remote(dsend.at[j], drecv.at[z], send_d.at[j], recv_d.at[z], at(j, y, x, u)).wait_send()

    spread_sent(low1, ebuf1, send_e, recv_e)
    spread_sent(low2, ebuf2, send_f, recv_f)


def on_device(telemetry, scales, bands, noise, start, target):
    vmem = pl.BlockSpec(memory_space=pltpu.VMEM)
    dma, gathers = pltpu.SemaphoreType.DMA, SHARDS + 16
    out = jax.ShapeDtypeStruct(target.shape[::-1], bf16)
    part = (HALF, ROWS)
    first, second = pl.pallas_call(
        kernel,
        out_shape=(out, out),
        in_specs=[vmem, vmem, pl.BlockSpec(memory_space=pltpu.SMEM), vmem, vmem, vmem],
        out_specs=(vmem, vmem),
        scratch_shapes=[
            pltpu.VMEM((ROWS, ROWS), bf16),
            pltpu.VMEM((SHARDS, ROWS, ROWS), bf16),
            pltpu.VMEM((PIECES, *part), bf16),
            pltpu.VMEM((PIECES * ROWS, HALF), bf16),
            pltpu.VMEM((PIECES * NL, 1, TILE), f32),
            pltpu.VMEM((TILES, PIECES * ROWS, TILE), bf16),
            pltpu.VMEM((TILES_SENSOR, ROWS, TILE), f32),
            pltpu.VMEM((PIECES * ROWS, HALF), f32),
            pltpu.VMEM((PIECES, *part), f32),
            pltpu.VMEM((PIECES, *part), f32),
            pltpu.VMEM((PIECES, *part), f32),
            pltpu.VMEM((PIECES, *part), f32),
            pltpu.VMEM(part, bf16),
            pltpu.VMEM((SLOTS, 8, ROWS), f32),
            pltpu.VMEM((8, ROWS), f32),
            pltpu.VMEM(part, bf16),
            pltpu.VMEM(part, bf16),
            pltpu.VMEM((SHARDS, *part), bf16),
            pltpu.VMEM((SLOTS, *part), bf16),
            pltpu.VMEM((SLOTS, *part), bf16),
            dma((gathers,)), dma((SHARDS,)),
            dma((NZ,)), dma((NZ,)),
            dma((8,)), dma,
            dma((8,)), dma,
            dma((NZ,)), dma((NZ,)),
            dma((gathers,)), dma((SHARDS,)),
            dma((NZ,)), dma((NZ,)),
            dma((SLOTS,)), dma((SLOTS,)),
            dma((SLOTS,)), dma((SLOTS,)),
        ],
        compiler_params=pltpu.CompilerParams(
            collective_id=0, has_side_effects=True, vmem_limit_bytes=60 * 2**20
        ),
    )(telemetry.T, scales.reshape(1, ROWS), bands, noise.reshape(SLOTS, ROWS), start.T, target.T)
    return first.T.astype(f32), second.T.astype(f32)


def solution(mesh):
    placed = (P(("col", "row"), None), P(("col", "row")), P(), P("row"), P(("col", "row"), None), P("row", None))
    return jax.shard_map(
        on_device,
        mesh=mesh,
        in_specs=placed,
        out_specs=(P("row", None), P("row", None)),
        check_vma=False,
    )
```

```python
import jax
import jax.numpy as jnp
from jax import lax
from jax.experimental import pallas as pl
from jax.experimental.pallas import tpu as pltpu
from jax.sharding import PartitionSpec as P

NZ, NH, NL, NX, NU = 8, 2, 4, 4, 2
NY = NH * NL
ROWS = 128
HALF = ROWS // 2
SUBAP = 2048
SHARDS = NY * NX * NU
PIECES = NZ
TILE = NU * ROWS
TILES = SHARDS // NU
TILES_SENSOR = SUBAP // TILE
SLOTS = 16
CHUNK = 4
MESH = pl.DeviceIdType.MESH
damping = 0.4
f32, bf16 = jnp.float32, jnp.bfloat16


def kernel(
    telemetry, scales, bands, noise, start, target, out1, out2,
    joined, colb, rowp, srow, inv, cov, dist, acc, bsend, brecv, dsend, drecv,
    tgt, noises, noi, low1, low2, cbuf, zbuf1, zbuf2, ebuf1, ebuf2,
    send_a, recv_a, send_r, recv_r, send_t, recv_t, send_n, recv_n, send_b, recv_b,
    send_c, recv_c, send_d, recv_d, send_g, recv_g, send_h, recv_h, send_e, recv_e, send_f, recv_f,
):
    row, col = lax.axis_index("row"), lax.axis_index("col")
    z, h = col // NH, col % NH
    l, x, u = row // (NX * NU), row // NU % NX, row % NU
    y = h * NL + l

    def rowid(yy, xx, uu):
        return yy % NL * (NX * NU) + xx * NU + uu

    def colid(zz, yy):
        return zz * NH + yy // NL

    def at(zz, yy, xx, uu):
        return rowid(yy, xx, uu), colid(zz, yy)

    def shard(yy, xx, uu):
        return (yy * NX + xx) * NU + uu

    def remote(src, dst, ssem, rsem, dev):
        return pltpu.make_async_remote_copy(
            src_ref=src, dst_ref=dst, send_sem=ssem, recv_sem=rsem, device_id=dev, device_id_type=MESH
        )

    def put_maybe_self(src, dst, ssem, rsem, dev):
        mine = (dev[0] == row) & (dev[1] == col)

        @pl.when(mine)
        def _():
            pltpu.make_async_copy(src, dst, rsem).start()

        @pl.when(jnp.logical_not(mine))
        def _():
            remote(src, dst, ssem, rsem, dev).start()

    me = shard(y, x, u)
    here = (row, col)
    xl, xr, xo = (x + NX - 1) % NX, (x + 1) % NX, (x + 2) % NX

    def near(i, start, size):
        return (start + i % 2 * ((i + 1) // 2) - (1 - i % 2) * (i // 2) + size) % size

    def y_of(i):
        return near(i, y, NY)

    def piece(i):
        return near(PIECES - 1 - i, z, NZ)

    zs = [near(i, z, NZ) for i in range(NZ - 1, 0, -1)]

    barrier = pltpu.get_barrier_semaphore()
    greet = [at(zz, y, x, u) for zz in zs] + [at(z, y_of(i), x, u) for i in range(1, NY)]
    greet += [at(z, y, xl, u), at(z, y, xr, u), at(z, y, x, 1 - u)]
    for dev in greet:
        pl.semaphore_signal(barrier, inc=1, device_id=dev, device_id_type=MESH)

    slopes = telemetry[...].astype(f32) * scales[...].astype(f32) * (1.0 / 128.0)
    joined[:HALF, :] = slopes.astype(bf16)
    joined[HALF:, :] = start[...]
    for s in range(SLOTS):
        noises[s] = jnp.broadcast_to(noise[s : s + 1, :], (8, ROWS))
    colb[me] = joined[...]
    rowp[z] = joined[:HALF, :]

    p0 = (l % 2 * (NX * NU) + x * NU + u) * ROWS
    base_d = (
        p0 + lax.broadcasted_iota(jnp.int32, (ROWS, TILE), 0) - lax.broadcasted_iota(jnp.int32, (ROWS, TILE), 1)
    )
    for t in range(TILES_SENSOR):
        dist[t] = jnp.abs(base_d - t * TILE).astype(f32)
    for i in range(PIECES):
        for k in range(NL):
            a, b = NL * piece(i) + y // 2, NL * z + k
            band = bands[jnp.minimum(a, b), jnp.maximum(a, b)].astype(f32)
            inv[i * NL + k] = 1.0 / jnp.full((1, TILE), band, f32)
    acc[...] = jnp.zeros_like(acc)
    pl.semaphore_wait(barrier, len(greet))

    left, right, other = at(z, y, xl, u), at(z, y, xr, u), at(z, y, x, 1 - u)

    def plane_gather(src, buf, ssem, rsem):
        def send(k, s_src, s, dev):
            remote(s_src, buf.at[s], ssem.at[k], rsem.at[s], dev).start()

        def wait(s):
            remote(src, buf.at[s], ssem.at[0], rsem.at[s], here).wait_recv()

        def begin():
            for i in range(NY - 1, 0, -1):
                send(i - 1, src, me, at(z, y_of(i), x, u))
            for k, dev in enumerate((left, right, other)):
                send(NY - 1 + k, src, me, dev)

        def y_step(i):
            s = shard(y_of(i), x, u)
            wait(s)
            for k, dev in enumerate((left, right, other)):
                send(NY - 1 + 3 * i + k, buf.at[s], s, dev)

        def x_step(i):
            yy = y_of(i)
            k = 4 * NY - 1 + 3 * i
            s = shard(yy, xl, u)
            wait(s)
            pl.when(yy % 2 == 0)(lambda s=s: send(k, buf.at[s], s, right))
            send(k + 1, buf.at[s], s, other)
            s = shard(yy, xr, u)
            wait(s)
            pl.when(yy % 2 == 1)(lambda s=s: send(k, buf.at[s], s, left))
            send(k + 2, buf.at[s], s, other)

        def o_step(i):
            s = shard(y_of(i), xo, u)
            wait(s)
            send(7 * NY - 1 + i, buf.at[s], s, other)

        def other_step(i):
            for xx in range(NX):
                wait(shard(y_of(i), xx, 1 - u))

        def paced(step):
            def relay(i, carry):
                pl.when(i < NY)(lambda: x_step(i))
                pl.when((i >= 1) & (i <= NY))(lambda: o_step(i - 1))

                @pl.when(i >= 2)
                def _():
                    other_step(i - 2)
                    step(i - 2)

                return carry

            lax.fori_loop(0, NY + 2, relay, 0)

        def drain():
            def one(k, carry):
                remote(src, buf.at[me], ssem.at[k], rsem.at[me], here).wait_send()
                return carry

            lax.fori_loop(0, 8 * NY - 1, one, 0)

        return begin, y_step, paced, drain

    mine_s = joined.at[pl.ds(0, HALF)]
    begin_a, y_step_a, paced_a, drain_a = plane_gather(joined, colb, send_a, recv_a)
    begin_a()
    for k, zz in enumerate(zs):
        remote(mine_s, rowp.at[z], send_r.at[k], recv_r.at[z], at(zz, y, x, u)).start()
    for i in range(1, NY):
        y_step_a(i)
    for zz in zs:
        remote(mine_s, rowp.at[zz], send_r.at[0], recv_r.at[zz], here).wait_recv()
    for i in range(PIECES):
        v = rowp[piece(i)].astype(f32) * (1.0 / 16384.0)
        srow[pl.ds(i * ROWS, ROWS), :] = jnp.transpose(v).astype(bf16)

    contract_last = (((1,), (1,)), ((), ()))
    slope_rows, panel_rows = slice(0, HALF), slice(HALF, ROWS)

    def wide(ref, t, part):
        return jnp.concatenate([ref[NU * t + i, part, :] for i in range(NX * NU)], axis=1)

    def rows_of(c):
        return pl.ds(c * CHUNK * ROWS, CHUNK * ROWS)

    def build(c, yy):
        span, t0 = rows_of(c), yy * NX
        entries = []
        for n in range(NX):
            cols = jnp.concatenate([colb[NU * (t0 + n) + i, slope_rows, :] for i in range(NU)], axis=1)
            raw = jnp.dot(srow[span, :], cols, preferred_element_type=f32)
            d = dist[yy % 2 * NX + n]
            parts = []
            for i in range(CHUNK):
                taper = jnp.maximum(0.0, 1.0 - d * inv[(c * CHUNK + i) * NL + yy // 2])
                parts.append((taper * raw[i * ROWS : (i + 1) * ROWS, :]).astype(bf16))
            entry = jnp.concatenate(parts, axis=0)
            cov[t0 + n, span, :] = entry
            entries.append(entry)
        acc[span, :] += lax.dot_general(
            jnp.concatenate(entries, axis=1), wide(colb, t0, panel_rows), contract_last, preferred_element_type=f32
        )

    def multiply(c, yy):
        span, t0 = rows_of(c), yy * NX
        entries = jnp.concatenate([cov[t0 + n, span, :] for n in range(NX)], axis=1)
        acc[span, :] += lax.dot_general(
            entries, wide(cbuf, t0, slice(None)), contract_last, preferred_element_type=f32
        )

    def send_rows(c, sbuf, rbuf, ssem, rsem):
        for i in range(c * CHUNK, (c + 1) * CHUNK):
            sbuf[i] = jnp.transpose(acc[pl.ds(i * ROWS, ROWS), :])
            if i < PIECES - 1:
                remote(sbuf.at[i], rbuf.at[z], ssem.at[i], rsem.at[z], at(piece(i), y, x, u)).start()

    def rest(c, step):
        def one(yy, carry):
            step(c, yy)
            return carry

        lax.fori_loop(0, NY, one, 0)

    paced_a(lambda i: build(0, y_of(i)))
    send_rows(0, bsend, brecv, send_b, recv_b)

    def target_part(slot):
        return target.at[:, pl.ds(pl.multiple_of(slot * ROWS, ROWS), ROWS)]

    source = (l == z // 2) & (x // 2 == z % 2)
    owner_dev = []
    for xx in range(NX):
        for uu in range(NU):
            slot = h * (NX * NU) + xx * NU + uu
            dev = ((2 * u + h) * (NX * NU) + xx * NU + uu, z * NH + x % NH)
            owner_dev.append((slot, dev))

    @pl.when(source)
    def _():
        for k, (slot, dev) in enumerate(owner_dev):
            put_maybe_self(target_part(slot), tgt, send_t.at[k], recv_t, dev)
            put_maybe_self(noises.at[slot], noi, send_n.at[k], recv_n, dev)

    for c in range(1, PIECES // CHUNK):
        rest(c, build)
        send_rows(c, bsend, brecv, send_b, recv_b)

    def collected(sbuf, rbuf, rsem):
        total = sbuf[PIECES - 1]
        for zz in zs:
            remote(sbuf.at[0], rbuf.at[zz], send_b.at[0], rsem.at[zz], here).wait_recv()
            total = total + rbuf[zz]
        return total

    remote(target_part(0), tgt, send_t.at[0], recv_t, here).wait_recv()
    remote(noises.at[0], noi, send_n.at[0], recv_n, here).wait_recv()
    s_own = joined[:HALF, :].astype(f32)
    x_own = joined[HALF:, :].astype(f32)
    raw_own = jnp.sum(s_own * s_own, axis=0, keepdims=True) * (1.0 / 16384.0)
    diag = raw_own + noi[0:1, :]
    weight = damping / diag
    extra = diag.astype(bf16).astype(f32) - raw_own.astype(bf16).astype(f32)
    tgt_own = tgt[...].astype(f32)

    first = x_own + weight * (tgt_own - (collected(bsend, brecv, recv_b) + extra * x_own))
    low1[...] = first.astype(bf16)

    slot_me = l % 2 * (NX * NU) + x * NU + u
    nearest = [near(i, z, NZ) for i in range(NZ)]

    def along_z(src, zbuf, ssem, rsem):
        for k, zz in enumerate(zs):
            remote(src, zbuf.at[z], ssem.at[k], rsem.at[z], at(zz, y, x, u)).start()
        zbuf[z] = src[...]

    def along_z_sent(src, zbuf, ssem, rsem):
        for k, zz in enumerate(zs):
            remote(src, zbuf.at[z], ssem.at[k], rsem.at[z], here).wait_send()

    def out_dev(zz, hh):
        return zz // 2 * (NX * NU) + (zz % 2 * 2 + h) * NU + l // 2, z * NH + hh

    def spread(src, zbuf, zsem, buf, ssem, rsem):
        for i, zz in enumerate(nearest):
            if i:
                remote(src, zbuf.at[zz], ssem.at[0], zsem.at[zz], here).wait_recv()
            for hh in range(NH):
                part = zbuf.at[zz] if i else src
                put_maybe_self(part, buf.at[slot_me], ssem.at[i * NH + hh], rsem.at[slot_me], out_dev(zz, hh))

    def spread_sent(src, buf, ssem, rsem):
        for i, zz in enumerate(nearest):
            for hh in range(NH):
                dev = out_dev(zz, hh)

                @pl.when(jnp.logical_not((dev[0] == row) & (dev[1] == col)))
                def _():
                    remote(src, buf.at[slot_me], ssem.at[i * NH + hh], rsem.at[slot_me], dev).wait_send()

    def unpack_out(src, buf, rsem, out):
        for s in range(SLOTS):
            remote(src, buf.at[s], send_e.at[0], rsem.at[s], here).wait_recv()
            out[:, pl.ds(s * ROWS, ROWS)] = buf[s]

    begin_c, y_step_c, paced_c, drain_c = plane_gather(low1, cbuf, send_c, recv_c)
    begin_c()
    along_z(low1, zbuf1, send_g, recv_g)
    cbuf[me] = low1[...]
    acc[...] = jnp.zeros_like(acc)
    for i in range(1, NY):
        y_step_c(i)
    paced_c(lambda i: multiply(0, y_of(i)))
    send_rows(0, dsend, drecv, send_d, recv_d)
    spread(low1, zbuf1, recv_g, ebuf1, send_e, recv_e)
    for c in range(1, PIECES // CHUNK):
        rest(c, multiply)
        send_rows(c, dsend, drecv, send_d, recv_d)

    product1 = collected(dsend, drecv, recv_d) + extra * first.astype(bf16).astype(f32)
    low2[...] = (first + weight * (tgt_own - product1)).astype(bf16)
    along_z(low2, zbuf2, send_h, recv_h)
    spread(low2, zbuf2, recv_h, ebuf2, send_f, recv_f)
    unpack_out(low1, ebuf1, recv_e, out1)
    unpack_out(low2, ebuf2, recv_f, out2)

    drain_a()
    drain_c()
    for k, zz in enumerate(zs):
        remote(mine_s, rowp.at[z], send_r.at[k], recv_r.at[z], at(zz, y, x, u)).wait_send()

    @pl.when(source)
    def _():
        for k, (slot, dev) in enumerate(owner_dev):
            @pl.when(jnp.logical_not((dev[0] == row) & (dev[1] == col)))
            def _():
                remote(target_part(slot), tgt, send_t.at[k], recv_t, dev).wait_send()
                remote(noises.at[slot], noi, send_n.at[k], recv_n, dev).wait_send()

    for i in range(PIECES - 1):
        remote(bsend.at[i], brecv.at[z], send_b.at[i], recv_b.at[z], here).wait_send()
        remote(dsend.at[i], drecv.at[z], send_d.at[i], recv_d.at[z], here).wait_send()

    along_z_sent(low1, zbuf1, send_g, recv_g)
    along_z_sent(low2, zbuf2, send_h, recv_h)
    spread_sent(low1, ebuf1, send_e, recv_e)
    spread_sent(low2, ebuf2, send_f, recv_f)


def on_device(telemetry, scales, bands, noise, start, target):
    vmem = pl.BlockSpec(memory_space=pltpu.VMEM)
    dma, gathers = pltpu.SemaphoreType.DMA, SHARDS
    out = jax.ShapeDtypeStruct(target.shape[::-1], bf16)
    part = (HALF, ROWS)
    first, second = pl.pallas_call(
        kernel,
        out_shape=(out, out),
        in_specs=[vmem, vmem, pl.BlockSpec(memory_space=pltpu.SMEM), vmem, vmem, vmem],
        out_specs=(vmem, vmem),
        scratch_shapes=[
            pltpu.VMEM((ROWS, ROWS), bf16),
            pltpu.VMEM((SHARDS, ROWS, ROWS), bf16),
            pltpu.VMEM((PIECES, *part), bf16),
            pltpu.VMEM((PIECES * ROWS, HALF), bf16),
            pltpu.VMEM((PIECES * NL, 1, TILE), f32),
            pltpu.VMEM((TILES, PIECES * ROWS, TILE), bf16),
            pltpu.VMEM((TILES_SENSOR, ROWS, TILE), f32),
            pltpu.VMEM((PIECES * ROWS, HALF), f32),
            pltpu.VMEM((PIECES, *part), f32),
            pltpu.VMEM((PIECES, *part), f32),
            pltpu.VMEM((PIECES, *part), f32),
            pltpu.VMEM((PIECES, *part), f32),
            pltpu.VMEM(part, bf16),
            pltpu.VMEM((SLOTS, 8, ROWS), f32),
            pltpu.VMEM((8, ROWS), f32),
            pltpu.VMEM(part, bf16),
            pltpu.VMEM(part, bf16),
            pltpu.VMEM((SHARDS, *part), bf16),
            pltpu.VMEM((NZ, *part), bf16),
            pltpu.VMEM((NZ, *part), bf16),
            pltpu.VMEM((SLOTS, *part), bf16),
            pltpu.VMEM((SLOTS, *part), bf16),
            dma((gathers,)), dma((SHARDS,)),
            dma((NZ,)), dma((NZ,)),
            dma((8,)), dma,
            dma((8,)), dma,
            dma((NZ,)), dma((NZ,)),
            dma((gathers,)), dma((SHARDS,)),
            dma((NZ,)), dma((NZ,)),
            dma((NZ,)), dma((NZ,)),
            dma((NZ,)), dma((NZ,)),
            dma((SLOTS,)), dma((SLOTS,)),
            dma((SLOTS,)), dma((SLOTS,)),
        ],
        compiler_params=pltpu.CompilerParams(
            collective_id=0, has_side_effects=True, vmem_limit_bytes=60 * 2**20
        ),
    )(telemetry.T, scales.reshape(1, ROWS), bands, noise.reshape(SLOTS, ROWS), start.T, target.T)
    return first.T.astype(f32), second.T.astype(f32)


def solution(mesh):
    placed = (P(("col", "row"), None), P(("col", "row")), P(), P("row"), P(("col", "row"), None), P("row", None))
    return jax.shard_map(
        on_device,
        mesh=mesh,
        in_specs=placed,
        out_specs=(P("row", None), P("row", None)),
        check_vma=False,
    )
```

```python
import jax
import jax.numpy as jnp
from jax import lax
from jax.experimental import pallas as pl
from jax.experimental.pallas import tpu as pltpu
from jax.sharding import PartitionSpec as P

NZ, NH, NL, NX, NU = 8, 2, 4, 4, 2
NY = NH * NL
ROWS = 128
HALF = ROWS // 2
SUBAP = 2048
SHARDS = NY * NX * NU
PIECES = NZ
TILE = NU * ROWS
TILES = SHARDS // NU
TILES_SENSOR = SUBAP // TILE
SLOTS = 16
CHUNK = 4
MESH = pl.DeviceIdType.MESH
damping = 0.4
f32, bf16 = jnp.float32, jnp.bfloat16


def kernel(
    telemetry, scales, bands, noise, start, target, out1, out2,
    joined, colb, rowp, srow, inv, cov, dist, acc, bsend, brecv, dsend, drecv,
    tgt, noises, noi, low1, low2, cbuf, zbuf1, zbuf2, ebuf1, ebuf2,
    send_a, recv_a, send_r, recv_r, send_t, recv_t, send_n, recv_n, send_b, recv_b,
    send_c, recv_c, send_d, recv_d, send_g, recv_g, send_h, recv_h, send_e, recv_e, send_f, recv_f,
):
    row, col = lax.axis_index("row"), lax.axis_index("col")
    z, h = col // NH, col % NH
    l, x, u = row // (NX * NU), row // NU % NX, row % NU
    y = h * NL + l

    def rowid(yy, xx, uu):
        return yy % NL * (NX * NU) + xx * NU + uu

    def colid(zz, yy):
        return zz * NH + yy // NL

    def at(zz, yy, xx, uu):
        return rowid(yy, xx, uu), colid(zz, yy)

    def shard(yy, xx, uu):
        return (yy * NX + xx) * NU + uu

    def remote(src, dst, ssem, rsem, dev):
        return pltpu.make_async_remote_copy(
            src_ref=src, dst_ref=dst, send_sem=ssem, recv_sem=rsem, device_id=dev, device_id_type=MESH
        )

    def put_maybe_self(src, dst, ssem, rsem, dev):
        mine = (dev[0] == row) & (dev[1] == col)

        @pl.when(mine)
        def _():
            pltpu.make_async_copy(src, dst, rsem).start()

        @pl.when(jnp.logical_not(mine))
        def _():
            remote(src, dst, ssem, rsem, dev).start()

    me = shard(y, x, u)
    here = (row, col)
    xl, xr, xo = (x + NX - 1) % NX, (x + 1) % NX, (x + 2) % NX

    def near(i, start, size):
        return (start + i % 2 * ((i + 1) // 2) - (1 - i % 2) * (i // 2) + size) % size

    def y_of(i):
        return near(i, y, NY)

    def piece(i):
        return near(PIECES - 1 - i, z, NZ)

    zs = [near(i, z, NZ) for i in range(NZ - 1, 0, -1)]

    barrier = pltpu.get_barrier_semaphore()
    greet = [at(zz, y, x, u) for zz in zs] + [at(z, y_of(i), x, u) for i in range(1, NY)]
    greet += [at(z, y, xl, u), at(z, y, xr, u), at(z, y, x, 1 - u)]
    for dev in greet:
        pl.semaphore_signal(barrier, inc=1, device_id=dev, device_id_type=MESH)

    slopes = telemetry[...].astype(f32) * scales[...].astype(f32) * (1.0 / 128.0)
    joined[:HALF, :] = slopes.astype(bf16)
    joined[HALF:, :] = start[...]
    for s in range(SLOTS):
        noises[s] = jnp.broadcast_to(noise[s : s + 1, :], (8, ROWS))
    colb[me] = joined[...]
    rowp[z] = joined[:HALF, :]

    p0 = (l % 2 * (NX * NU) + x * NU + u) * ROWS
    base_d = (
        p0 + lax.broadcasted_iota(jnp.int32, (ROWS, TILE), 0) - lax.broadcasted_iota(jnp.int32, (ROWS, TILE), 1)
    )
    for t in range(TILES_SENSOR):
        dist[t] = jnp.abs(base_d - t * TILE).astype(f32)
    for i in range(PIECES):
        for k in range(NL):
            a, b = NL * piece(i) + y // 2, NL * z + k
            band = bands[jnp.minimum(a, b), jnp.maximum(a, b)].astype(f32)
            inv[i * NL + k] = 1.0 / jnp.full((1, TILE), band, f32)
    acc[...] = jnp.zeros_like(acc)
    pl.semaphore_wait(barrier, len(greet))

    left, right, other = at(z, y, xl, u), at(z, y, xr, u), at(z, y, x, 1 - u)

    def plane_gather(src, buf, ssem, rsem):
        def send(k, s_src, s, dev):
            remote(s_src, buf.at[s], ssem.at[k], rsem.at[s], dev).start()

        def wait(s):
            remote(src, buf.at[s], ssem.at[0], rsem.at[s], here).wait_recv()

        def begin():
            for i in range(NY - 1, 0, -1):
                send(i - 1, src, me, at(z, y_of(i), x, u))
            for k, dev in enumerate((left, right, other)):
                send(NY - 1 + k, src, me, dev)

        def y_step(i):
            s = shard(y_of(i), x, u)
            wait(s)
            for k, dev in enumerate((left, right, other)):
                send(NY - 1 + 3 * i + k, buf.at[s], s, dev)

        def x_step(i):
            yy = y_of(i)
            k = 4 * NY - 1 + 3 * i
            s = shard(yy, xl, u)
            wait(s)
            pl.when(yy % 2 == 0)(lambda s=s: send(k, buf.at[s], s, right))
            send(k + 1, buf.at[s], s, other)
            s = shard(yy, xr, u)
            wait(s)
            pl.when(yy % 2 == 1)(lambda s=s: send(k, buf.at[s], s, left))
            send(k + 2, buf.at[s], s, other)

        def o_step(i):
            s = shard(y_of(i), xo, u)
            wait(s)
            send(7 * NY - 1 + i, buf.at[s], s, other)

        def other_step(i):
            for xx in range(NX):
                wait(shard(y_of(i), xx, 1 - u))

        def paced(step):
            def across(i, carry):
                x_step(i)
                return carry

            def relay(i, carry):
                pl.when(i < NY)(lambda: o_step(i))

                @pl.when(i >= 1)
                def _():
                    other_step(i - 1)
                    step(i - 1)

                return carry

            lax.fori_loop(0, NY, across, 0)
            lax.fori_loop(0, NY + 1, relay, 0)

        def drain():
            def one(k, carry):
                remote(src, buf.at[me], ssem.at[k], rsem.at[me], here).wait_send()
                return carry

            lax.fori_loop(0, 8 * NY - 1, one, 0)

        return begin, y_step, paced, drain

    mine_s = joined.at[pl.ds(0, HALF)]
    begin_a, y_step_a, paced_a, drain_a = plane_gather(joined, colb, send_a, recv_a)
    begin_a()
    for k, zz in enumerate(zs):
        remote(mine_s, rowp.at[z], send_r.at[k], recv_r.at[z], at(zz, y, x, u)).start()
    for i in range(1, NY):
        y_step_a(i)
    for zz in zs:
        remote(mine_s, rowp.at[zz], send_r.at[0], recv_r.at[zz], here).wait_recv()
    for i in range(PIECES):
        v = rowp[piece(i)].astype(f32) * (1.0 / 16384.0)
        srow[pl.ds(i * ROWS, ROWS), :] = jnp.transpose(v).astype(bf16)

    contract_last = (((1,), (1,)), ((), ()))
    slope_rows, panel_rows = slice(0, HALF), slice(HALF, ROWS)

    def wide(ref, t, part):
        return jnp.concatenate([ref[NU * t + i, part, :] for i in range(NX * NU)], axis=1)

    def rows_of(c):
        return pl.ds(c * CHUNK * ROWS, CHUNK * ROWS)

    def build(c, yy):
        span, t0 = rows_of(c), yy * NX
        entries = []
        for n in range(NX):
            cols = jnp.concatenate([colb[NU * (t0 + n) + i, slope_rows, :] for i in range(NU)], axis=1)
            raw = jnp.dot(srow[span, :], cols, preferred_element_type=f32)
            d = dist[yy % 2 * NX + n]
            parts = []
            for i in range(CHUNK):
                taper = jnp.maximum(0.0, 1.0 - d * inv[(c * CHUNK + i) * NL + yy // 2])
                parts.append((taper * raw[i * ROWS : (i + 1) * ROWS, :]).astype(bf16))
            entry = jnp.concatenate(parts, axis=0)
            cov[t0 + n, span, :] = entry
            entries.append(entry)
        acc[span, :] += lax.dot_general(
            jnp.concatenate(entries, axis=1), wide(colb, t0, panel_rows), contract_last, preferred_element_type=f32
        )

    def multiply(c, yy):
        span, t0 = rows_of(c), yy * NX
        entries = jnp.concatenate([cov[t0 + n, span, :] for n in range(NX)], axis=1)
        acc[span, :] += lax.dot_general(
            entries, wide(cbuf, t0, slice(None)), contract_last, preferred_element_type=f32
        )

    def send_rows(c, sbuf, rbuf, ssem, rsem):
        for i in range(c * CHUNK, (c + 1) * CHUNK):
            sbuf[i] = jnp.transpose(acc[pl.ds(i * ROWS, ROWS), :])
            if i < PIECES - 1:
                remote(sbuf.at[i], rbuf.at[z], ssem.at[i], rsem.at[z], at(piece(i), y, x, u)).start()

    def rest(c, step):
        def one(yy, carry):
            step(c, yy)
            return carry

        lax.fori_loop(0, NY, one, 0)

    paced_a(lambda i: build(0, y_of(i)))
    send_rows(0, bsend, brecv, send_b, recv_b)

    def target_part(slot):
        return target.at[:, pl.ds(pl.multiple_of(slot * ROWS, ROWS), ROWS)]

    source = (l == z // 2) & (x // 2 == z % 2)
    owner_dev = []
    for xx in range(NX):
        for uu in range(NU):
            slot = h * (NX * NU) + xx * NU + uu
            dev = ((2 * u + h) * (NX * NU) + xx * NU + uu, z * NH + x % NH)
            owner_dev.append((slot, dev))

    @pl.when(source)
    def _():
        for k, (slot, dev) in enumerate(owner_dev):
            put_maybe_self(target_part(slot), tgt, send_t.at[k], recv_t, dev)
            put_maybe_self(noises.at[slot], noi, send_n.at[k], recv_n, dev)

    for c in range(1, PIECES // CHUNK):
        rest(c, build)
        send_rows(c, bsend, brecv, send_b, recv_b)

    def collected(sbuf, rbuf, rsem):
        total = sbuf[PIECES - 1]
        for zz in zs:
            remote(sbuf.at[0], rbuf.at[zz], send_b.at[0], rsem.at[zz], here).wait_recv()
            total = total + rbuf[zz]
        return total

    remote(target_part(0), tgt, send_t.at[0], recv_t, here).wait_recv()
    remote(noises.at[0], noi, send_n.at[0], recv_n, here).wait_recv()
    s_own = joined[:HALF, :].astype(f32)
    x_own = joined[HALF:, :].astype(f32)
    raw_own = jnp.sum(s_own * s_own, axis=0, keepdims=True) * (1.0 / 16384.0)
    diag = raw_own + noi[0:1, :]
    weight = damping / diag
    extra = diag.astype(bf16).astype(f32) - raw_own.astype(bf16).astype(f32)
    tgt_own = tgt[...].astype(f32)

    first = x_own + weight * (tgt_own - (collected(bsend, brecv, recv_b) + extra * x_own))
    low1[...] = first.astype(bf16)

    slot_me = l % 2 * (NX * NU) + x * NU + u
    nearest = [near(i, z, NZ) for i in range(NZ)]

    def along_z(src, zbuf, ssem, rsem):
        for k, zz in enumerate(zs):
            remote(src, zbuf.at[z], ssem.at[k], rsem.at[z], at(zz, y, x, u)).start()
        zbuf[z] = src[...]

    def along_z_sent(src, zbuf, ssem, rsem):
        for k, zz in enumerate(zs):
            remote(src, zbuf.at[z], ssem.at[k], rsem.at[z], here).wait_send()

    def out_dev(zz, hh):
        return zz // 2 * (NX * NU) + (zz % 2 * 2 + h) * NU + l // 2, z * NH + hh

    def spread(src, zbuf, zsem, buf, ssem, rsem):
        for i, zz in enumerate(nearest):
            if i:
                remote(src, zbuf.at[zz], ssem.at[0], zsem.at[zz], here).wait_recv()
            for hh in range(NH):
                part = zbuf.at[zz] if i else src
                put_maybe_self(part, buf.at[slot_me], ssem.at[i * NH + hh], rsem.at[slot_me], out_dev(zz, hh))

    def spread_sent(src, buf, ssem, rsem):
        for i, zz in enumerate(nearest):
            for hh in range(NH):
                dev = out_dev(zz, hh)

                @pl.when(jnp.logical_not((dev[0] == row) & (dev[1] == col)))
                def _():
                    remote(src, buf.at[slot_me], ssem.at[i * NH + hh], rsem.at[slot_me], dev).wait_send()

    def unpack_out(src, buf, rsem, out):
        for s in range(SLOTS):
            remote(src, buf.at[s], send_e.at[0], rsem.at[s], here).wait_recv()
            out[:, pl.ds(s * ROWS, ROWS)] = buf[s]

    begin_c, y_step_c, paced_c, drain_c = plane_gather(low1, cbuf, send_c, recv_c)
    begin_c()
    along_z(low1, zbuf1, send_g, recv_g)
    cbuf[me] = low1[...]
    acc[...] = jnp.zeros_like(acc)
    for i in range(1, NY):
        y_step_c(i)
    paced_c(lambda i: multiply(0, y_of(i)))
    send_rows(0, dsend, drecv, send_d, recv_d)
    spread(low1, zbuf1, recv_g, ebuf1, send_e, recv_e)
    for c in range(1, PIECES // CHUNK):
        rest(c, multiply)
        send_rows(c, dsend, drecv, send_d, recv_d)

    product1 = collected(dsend, drecv, recv_d) + extra * first.astype(bf16).astype(f32)
    low2[...] = (first + weight * (tgt_own - product1)).astype(bf16)
    along_z(low2, zbuf2, send_h, recv_h)
    spread(low2, zbuf2, recv_h, ebuf2, send_f, recv_f)
    unpack_out(low1, ebuf1, recv_e, out1)
    unpack_out(low2, ebuf2, recv_f, out2)

    drain_a()
    drain_c()
    for k, zz in enumerate(zs):
        remote(mine_s, rowp.at[z], send_r.at[k], recv_r.at[z], at(zz, y, x, u)).wait_send()

    @pl.when(source)
    def _():
        for k, (slot, dev) in enumerate(owner_dev):
            @pl.when(jnp.logical_not((dev[0] == row) & (dev[1] == col)))
            def _():
                remote(target_part(slot), tgt, send_t.at[k], recv_t, dev).wait_send()
                remote(noises.at[slot], noi, send_n.at[k], recv_n, dev).wait_send()

    for i in range(PIECES - 1):
        remote(bsend.at[i], brecv.at[z], send_b.at[i], recv_b.at[z], here).wait_send()
        remote(dsend.at[i], drecv.at[z], send_d.at[i], recv_d.at[z], here).wait_send()

    along_z_sent(low1, zbuf1, send_g, recv_g)
    along_z_sent(low2, zbuf2, send_h, recv_h)
    spread_sent(low1, ebuf1, send_e, recv_e)
    spread_sent(low2, ebuf2, send_f, recv_f)


def on_device(telemetry, scales, bands, noise, start, target):
    vmem = pl.BlockSpec(memory_space=pltpu.VMEM)
    dma, gathers = pltpu.SemaphoreType.DMA, SHARDS
    out = jax.ShapeDtypeStruct(target.shape[::-1], bf16)
    part = (HALF, ROWS)
    first, second = pl.pallas_call(
        kernel,
        out_shape=(out, out),
        in_specs=[vmem, vmem, pl.BlockSpec(memory_space=pltpu.SMEM), vmem, vmem, pl.BlockSpec(memory_space=pl.ANY)],
        out_specs=(vmem, vmem),
        scratch_shapes=[
            pltpu.VMEM((ROWS, ROWS), bf16),
            pltpu.VMEM((SHARDS, ROWS, ROWS), bf16),
            pltpu.VMEM((PIECES, *part), bf16),
            pltpu.VMEM((PIECES * ROWS, HALF), bf16),
            pltpu.VMEM((PIECES * NL, 1, TILE), f32),
            pltpu.VMEM((TILES, PIECES * ROWS, TILE), bf16),
            pltpu.VMEM((TILES_SENSOR, ROWS, TILE), f32),
            pltpu.VMEM((PIECES * ROWS, HALF), f32),
            pltpu.VMEM((PIECES, *part), f32),
            pltpu.VMEM((PIECES, *part), f32),
            pltpu.VMEM((PIECES, *part), f32),
            pltpu.VMEM((PIECES, *part), f32),
            pltpu.VMEM(part, bf16),
            pltpu.VMEM((SLOTS, 8, ROWS), f32),
            pltpu.VMEM((8, ROWS), f32),
            pltpu.VMEM(part, bf16),
            pltpu.VMEM(part, bf16),
            pltpu.VMEM((SHARDS, *part), bf16),
            pltpu.VMEM((NZ, *part), bf16),
            pltpu.VMEM((NZ, *part), bf16),
            pltpu.VMEM((SLOTS, *part), bf16),
            pltpu.VMEM((SLOTS, *part), bf16),
            dma((gathers,)), dma((SHARDS,)),
            dma((NZ,)), dma((NZ,)),
            dma((8,)), dma,
            dma((8,)), dma,
            dma((NZ,)), dma((NZ,)),
            dma((gathers,)), dma((SHARDS,)),
            dma((NZ,)), dma((NZ,)),
            dma((NZ,)), dma((NZ,)),
            dma((NZ,)), dma((NZ,)),
            dma((SLOTS,)), dma((SLOTS,)),
            dma((SLOTS,)), dma((SLOTS,)),
        ],
        compiler_params=pltpu.CompilerParams(
            collective_id=0, has_side_effects=True, vmem_limit_bytes=60 * 2**20
        ),
    )(telemetry.T, scales.reshape(1, ROWS), bands, noise.reshape(SLOTS, ROWS), start.T, target.T)
    return first.T.astype(f32), second.T.astype(f32)


def solution(mesh):
    placed = (P(("col", "row"), None), P(("col", "row")), P(), P("row"), P(("col", "row"), None), P("row", None))
    return jax.shard_map(
        on_device,
        mesh=mesh,
        in_specs=placed,
        out_specs=(P("row", None), P("row", None)),
        check_vma=False,
    )
```

```python
import jax
import jax.numpy as jnp
from jax import lax
from jax.experimental import pallas as pl
from jax.experimental.pallas import tpu as pltpu
from jax.sharding import PartitionSpec as P

NZ, NH, NL, NX, NU = 8, 2, 4, 4, 2
NY = NH * NL
ROWS = 128
HALF = ROWS // 2
SUBAP = 2048
SHARDS = NY * NX * NU
PIECES = NZ
TILE = NU * ROWS
TILES = SHARDS // NU
TILES_SENSOR = SUBAP // TILE
SLOTS = 16
CHUNK = 4
AHEAD = 3
MESH = pl.DeviceIdType.MESH
damping = 0.4
f32, bf16 = jnp.float32, jnp.bfloat16


def kernel(
    telemetry, scales, bands, noise, start, target, out1, out2,
    joined, colb, rowp, srow, inv, cov, dist, acc, bsend, brecv, dsend, drecv,
    tgt, noises, noi, low1, low2, cbuf, zbuf1, zbuf2, ebuf1, ebuf2,
    send_a, recv_a, send_r, recv_r, send_t, recv_t, send_n, recv_n, send_b, recv_b,
    send_c, recv_c, send_d, recv_d, send_g, recv_g, send_h, recv_h, send_e, recv_e, send_f, recv_f,
):
    row, col = lax.axis_index("row"), lax.axis_index("col")
    z, h = col // NH, col % NH
    l, x, u = row // (NX * NU), row // NU % NX, row % NU
    y = h * NL + l

    def rowid(yy, xx, uu):
        return yy % NL * (NX * NU) + xx * NU + uu

    def colid(zz, yy):
        return zz * NH + yy // NL

    def at(zz, yy, xx, uu):
        return rowid(yy, xx, uu), colid(zz, yy)

    def shard(yy, xx, uu):
        return (yy * NX + xx) * NU + uu

    def remote(src, dst, ssem, rsem, dev):
        return pltpu.make_async_remote_copy(
            src_ref=src, dst_ref=dst, send_sem=ssem, recv_sem=rsem, device_id=dev, device_id_type=MESH
        )

    def put_maybe_self(src, dst, ssem, rsem, dev):
        mine = (dev[0] == row) & (dev[1] == col)

        @pl.when(mine)
        def _():
            pltpu.make_async_copy(src, dst, rsem).start()

        @pl.when(jnp.logical_not(mine))
        def _():
            remote(src, dst, ssem, rsem, dev).start()

    me = shard(y, x, u)
    here = (row, col)
    xl, xr, xo = (x + NX - 1) % NX, (x + 1) % NX, (x + 2) % NX

    def near(i, start, size):
        return (start + i % 2 * ((i + 1) // 2) - (1 - i % 2) * (i // 2) + size) % size

    def y_of(i):
        return near(i, y, NY)

    def piece(i):
        return near(PIECES - 1 - i, z, NZ)

    zs = [near(i, z, NZ) for i in range(NZ - 1, 0, -1)]

    barrier = pltpu.get_barrier_semaphore()
    greet = [at(zz, y, x, u) for zz in zs] + [at(z, y_of(i), x, u) for i in range(1, NY)]
    greet += [at(z, y, xl, u), at(z, y, xr, u), at(z, y, xo, u), at(z, y, x, 1 - u)]
    for dev in greet:
        pl.semaphore_signal(barrier, inc=1, device_id=dev, device_id_type=MESH)

    slopes = telemetry[...].astype(f32) * scales[...].astype(f32) * (1.0 / 128.0)
    joined[:HALF, :] = slopes.astype(bf16)
    joined[HALF:, :] = start[...]
    for s in range(SLOTS):
        noises[s] = jnp.broadcast_to(noise[s : s + 1, :], (8, ROWS))
    colb[me] = joined[...]
    rowp[z] = joined[:HALF, :]

    p0 = (l % 2 * (NX * NU) + x * NU + u) * ROWS
    base_d = (
        p0 + lax.broadcasted_iota(jnp.int32, (ROWS, TILE), 0) - lax.broadcasted_iota(jnp.int32, (ROWS, TILE), 1)
    )
    for t in range(TILES_SENSOR):
        dist[t] = jnp.abs(base_d - t * TILE).astype(f32)
    for i in range(PIECES):
        for k in range(NL):
            a, b = NL * piece(i) + y // 2, NL * z + k
            band = bands[jnp.minimum(a, b), jnp.maximum(a, b)].astype(f32)
            inv[i * NL + k] = 1.0 / jnp.full((1, TILE), band, f32)
    acc[...] = jnp.zeros_like(acc)
    pl.semaphore_wait(barrier, len(greet))

    other = at(z, y, x, 1 - u)
    across = [at(z, y, xo, u), at(z, y, xl, u), at(z, y, xr, u)]

    def plane_gather(src, buf, ssem, rsem):
        def send(k, s_src, s, dev):
            remote(s_src, buf.at[s], ssem.at[k], rsem.at[s], dev).start()

        def wait(s):
            remote(src, buf.at[s], ssem.at[0], rsem.at[s], here).wait_recv()

        def begin(beside):
            send(NY - 1 + len(across), src, me, other)
            for i in range(1, NY):
                send(i - 1, src, me, at(z, y_of(i), x, u))
                if i <= len(across):
                    send(NY - 2 + i, src, me, across[i - 1])
                beside(i)

        def y_step(i):
            s = shard(y_of(i), x, u)
            wait(s)
            for k, dev in enumerate((*across, other)):
                send(NY - 1 + NX * i + k, buf.at[s], s, dev)

        def x_step(i):
            for k, xx in enumerate((xl, xr, xo)):
                s = shard(y_of(i), xx, u)
                wait(s)
                send((1 + NX) * NY - 1 + (NX - 1) * i + k, buf.at[s], s, other)

        def other_step(i):
            for xx in range(NX):
                wait(shard(y_of(i), xx, 1 - u))

        def paced(step):
            def relay(i, carry):
                pl.when(i < NY)(lambda: x_step(i))

                @pl.when(i >= AHEAD)
                def _():
                    other_step(i - AHEAD)
                    step(i - AHEAD)

                return carry

            lax.fori_loop(0, NY + AHEAD, relay, 0)

        def drain():
            def one(k, carry):
                remote(src, buf.at[me], ssem.at[k], rsem.at[me], here).wait_send()
                return carry

            lax.fori_loop(0, 8 * NY - 1, one, 0)

        return begin, y_step, paced, drain

    mine_s = joined.at[pl.ds(0, HALF)]
    begin_a, y_step_a, paced_a, drain_a = plane_gather(joined, colb, send_a, recv_a)
    begin_a(lambda i: remote(mine_s, rowp.at[z], send_r.at[i], recv_r.at[z], at(near(i, z, NZ), y, x, u)).start())
    for i in range(1, NY):
        y_step_a(i)
    for zz in zs:
        remote(mine_s, rowp.at[zz], send_r.at[0], recv_r.at[zz], here).wait_recv()
    for i in range(PIECES):
        v = rowp[piece(i)].astype(f32) * (1.0 / 16384.0)
        srow[pl.ds(i * ROWS, ROWS), :] = jnp.transpose(v).astype(bf16)

    contract_last = (((1,), (1,)), ((), ()))
    slope_rows, panel_rows = slice(0, HALF), slice(HALF, ROWS)

    def wide(ref, t, part):
        return jnp.concatenate([ref[NU * t + i, part, :] for i in range(NX * NU)], axis=1)

    def rows_of(c):
        return pl.ds(c * CHUNK * ROWS, CHUNK * ROWS)

    def build(c, yy):
        span, t0 = rows_of(c), yy * NX
        entries = []
        for n in range(NX):
            cols = jnp.concatenate([colb[NU * (t0 + n) + i, slope_rows, :] for i in range(NU)], axis=1)
            raw = jnp.dot(srow[span, :], cols, preferred_element_type=f32)
            d = dist[yy % 2 * NX + n]
            parts = []
            for i in range(CHUNK):
                taper = jnp.maximum(0.0, 1.0 - d * inv[(c * CHUNK + i) * NL + yy // 2])
                parts.append((taper * raw[i * ROWS : (i + 1) * ROWS, :]).astype(bf16))
            entry = jnp.concatenate(parts, axis=0)
            cov[t0 + n, span, :] = entry
            entries.append(entry)
        acc[span, :] += lax.dot_general(
            jnp.concatenate(entries, axis=1), wide(colb, t0, panel_rows), contract_last, preferred_element_type=f32
        )

    def multiply(c, yy):
        span, t0 = rows_of(c), yy * NX
        entries = jnp.concatenate([cov[t0 + n, span, :] for n in range(NX)], axis=1)
        acc[span, :] += lax.dot_general(
            entries, wide(cbuf, t0, slice(None)), contract_last, preferred_element_type=f32
        )

    def send_rows(c, sbuf, rbuf, ssem, rsem):
        for i in range(c * CHUNK, (c + 1) * CHUNK):
            sbuf[i] = jnp.transpose(acc[pl.ds(i * ROWS, ROWS), :])
            if i < PIECES - 1:
                remote(sbuf.at[i], rbuf.at[z], ssem.at[i], rsem.at[z], at(piece(i), y, x, u)).start()

    def rest(step):
        def one(yy, carry):
            step(1, yy)
            return carry

        lax.fori_loop(0, NY, one, 0)

    paced_a(lambda i: build(0, y_of(i)))
    send_rows(0, bsend, brecv, send_b, recv_b)

    def target_part(slot):
        return target.at[:, pl.ds(pl.multiple_of(slot * ROWS, ROWS), ROWS)]

    source = (l == z // 2) & (x // 2 == z % 2)
    owner_dev = []
    for xx in range(NX):
        for uu in range(NU):
            slot = h * (NX * NU) + xx * NU + uu
            dev = ((2 * u + h) * (NX * NU) + xx * NU + uu, z * NH + x % NH)
            owner_dev.append((slot, dev))

    @pl.when(source)
    def _():
        for k, (slot, dev) in enumerate(owner_dev):
            put_maybe_self(target_part(slot), tgt, send_t.at[k], recv_t, dev)
            put_maybe_self(noises.at[slot], noi, send_n.at[k], recv_n, dev)

    rest(build)
    send_rows(1, bsend, brecv, send_b, recv_b)

    def collected(sbuf, rbuf, rsem):
        total = sbuf[PIECES - 1]
        for zz in zs:
            remote(sbuf.at[0], rbuf.at[zz], send_b.at[0], rsem.at[zz], here).wait_recv()
            total = total + rbuf[zz]
        return total

    remote(target_part(0), tgt, send_t.at[0], recv_t, here).wait_recv()
    remote(noises.at[0], noi, send_n.at[0], recv_n, here).wait_recv()
    s_own = joined[:HALF, :].astype(f32)
    x_own = joined[HALF:, :].astype(f32)
    raw_own = jnp.sum(s_own * s_own, axis=0, keepdims=True) * (1.0 / 16384.0)
    diag = raw_own + noi[0:1, :]
    weight = damping / diag
    extra = diag.astype(bf16).astype(f32) - raw_own.astype(bf16).astype(f32)
    tgt_own = tgt[...].astype(f32)

    first = x_own + weight * (tgt_own - (collected(bsend, brecv, recv_b) + extra * x_own))
    low1[...] = first.astype(bf16)

    slot_me = l % 2 * (NX * NU) + x * NU + u
    nearest = [near(i, z, NZ) for i in range(NZ)]

    def along_z(src, zbuf, ssem, rsem, i):
        remote(src, zbuf.at[z], ssem.at[i], rsem.at[z], at(near(i, z, NZ), y, x, u)).start()

    def along_z_sent(src, zbuf, ssem, rsem):
        for i in range(1, NZ):
            remote(src, zbuf.at[z], ssem.at[i], rsem.at[z], here).wait_send()

    def out_dev(zz, hh):
        return zz // 2 * (NX * NU) + (zz % 2 * 2 + h) * NU + l // 2, z * NH + hh

    def spread(src, zbuf, zsem, buf, ssem, rsem):
        for i, zz in enumerate(nearest):
            if i:
                remote(src, zbuf.at[zz], ssem.at[0], zsem.at[zz], here).wait_recv()
            for hh in range(NH):
                part = zbuf.at[zz] if i else src
                put_maybe_self(part, buf.at[slot_me], ssem.at[i * NH + hh], rsem.at[slot_me], out_dev(zz, hh))

    def spread_sent(src, buf, ssem, rsem):
        for i, zz in enumerate(nearest):
            for hh in range(NH):
                dev = out_dev(zz, hh)

                @pl.when(jnp.logical_not((dev[0] == row) & (dev[1] == col)))
                def _():
                    remote(src, buf.at[slot_me], ssem.at[i * NH + hh], rsem.at[slot_me], dev).wait_send()

    def unpack_out(src, buf, rsem, out):
        for s in range(SLOTS):
            remote(src, buf.at[s], send_e.at[0], rsem.at[s], here).wait_recv()
            out[:, pl.ds(s * ROWS, ROWS)] = buf[s]

    begin_c, y_step_c, paced_c, drain_c = plane_gather(low1, cbuf, send_c, recv_c)
    begin_c(lambda i: along_z(low1, zbuf1, send_g, recv_g, i))
    cbuf[me] = low1[...]
    acc[...] = jnp.zeros_like(acc)
    for i in range(1, NY):
        y_step_c(i)
    paced_c(lambda i: multiply(0, y_of(i)))
    send_rows(0, dsend, drecv, send_d, recv_d)
    spread(low1, zbuf1, recv_g, ebuf1, send_e, recv_e)
    rest(multiply)
    send_rows(1, dsend, drecv, send_d, recv_d)

    product1 = collected(dsend, drecv, recv_d) + extra * first.astype(bf16).astype(f32)
    low2[...] = (first + weight * (tgt_own - product1)).astype(bf16)
    for i in range(NZ - 1, 0, -1):
        along_z(low2, zbuf2, send_h, recv_h, i)
    spread(low2, zbuf2, recv_h, ebuf2, send_f, recv_f)
    unpack_out(low1, ebuf1, recv_e, out1)
    unpack_out(low2, ebuf2, recv_f, out2)

    drain_a()
    drain_c()
    for i in range(1, NZ):
        remote(mine_s, rowp.at[z], send_r.at[i], recv_r.at[z], here).wait_send()

    @pl.when(source)
    def _():
        for k, (slot, dev) in enumerate(owner_dev):
            @pl.when(jnp.logical_not((dev[0] == row) & (dev[1] == col)))
            def _():
                remote(target_part(slot), tgt, send_t.at[k], recv_t, dev).wait_send()
                remote(noises.at[slot], noi, send_n.at[k], recv_n, dev).wait_send()

    for i in range(PIECES - 1):
        remote(bsend.at[i], brecv.at[z], send_b.at[i], recv_b.at[z], here).wait_send()
        remote(dsend.at[i], drecv.at[z], send_d.at[i], recv_d.at[z], here).wait_send()

    along_z_sent(low1, zbuf1, send_g, recv_g)
    along_z_sent(low2, zbuf2, send_h, recv_h)
    spread_sent(low1, ebuf1, send_e, recv_e)
    spread_sent(low2, ebuf2, send_f, recv_f)


def on_device(telemetry, scales, bands, noise, start, target):
    vmem = pl.BlockSpec(memory_space=pltpu.VMEM)
    dma, gathers = pltpu.SemaphoreType.DMA, SHARDS
    out = jax.ShapeDtypeStruct(target.shape[::-1], bf16)
    part = (HALF, ROWS)
    first, second = pl.pallas_call(
        kernel,
        out_shape=(out, out),
        in_specs=[vmem, vmem, pl.BlockSpec(memory_space=pltpu.SMEM), vmem, vmem, pl.BlockSpec(memory_space=pl.ANY)],
        out_specs=(vmem, vmem),
        scratch_shapes=[
            pltpu.VMEM((ROWS, ROWS), bf16),
            pltpu.VMEM((SHARDS, ROWS, ROWS), bf16),
            pltpu.VMEM((PIECES, *part), bf16),
            pltpu.VMEM((PIECES * ROWS, HALF), bf16),
            pltpu.VMEM((PIECES * NL, 1, TILE), f32),
            pltpu.VMEM((TILES, PIECES * ROWS, TILE), bf16),
            pltpu.VMEM((TILES_SENSOR, ROWS, TILE), f32),
            pltpu.VMEM((PIECES * ROWS, HALF), f32),
            pltpu.VMEM((PIECES, *part), f32),
            pltpu.VMEM((PIECES, *part), f32),
            pltpu.VMEM((PIECES, *part), f32),
            pltpu.VMEM((PIECES, *part), f32),
            pltpu.VMEM(part, bf16),
            pltpu.VMEM((SLOTS, 8, ROWS), f32),
            pltpu.VMEM((8, ROWS), f32),
            pltpu.VMEM(part, bf16),
            pltpu.VMEM(part, bf16),
            pltpu.VMEM((SHARDS, *part), bf16),
            pltpu.VMEM((NZ, *part), bf16),
            pltpu.VMEM((NZ, *part), bf16),
            pltpu.VMEM((SLOTS, *part), bf16),
            pltpu.VMEM((SLOTS, *part), bf16),
            dma((gathers,)), dma((SHARDS,)),
            dma((NZ,)), dma((NZ,)),
            dma((8,)), dma,
            dma((8,)), dma,
            dma((NZ,)), dma((NZ,)),
            dma((gathers,)), dma((SHARDS,)),
            dma((NZ,)), dma((NZ,)),
            dma((NZ,)), dma((NZ,)),
            dma((NZ,)), dma((NZ,)),
            dma((SLOTS,)), dma((SLOTS,)),
            dma((SLOTS,)), dma((SLOTS,)),
        ],
        compiler_params=pltpu.CompilerParams(
            collective_id=0, has_side_effects=True, vmem_limit_bytes=60 * 2**20
        ),
    )(telemetry.T, scales.reshape(1, ROWS), bands, noise.reshape(SLOTS, ROWS), start.T, target.T)
    return first.T.astype(f32), second.T.astype(f32)


def solution(mesh):
    placed = (P(("col", "row"), None), P(("col", "row")), P(), P("row"), P(("col", "row"), None), P("row", None))
    return jax.shard_map(
        on_device,
        mesh=mesh,
        in_specs=placed,
        out_specs=(P("row", None), P("row", None)),
        check_vma=False,
    )
```

```python
import jax
import jax.numpy as jnp
from jax import lax
from jax.experimental import pallas as pl
from jax.experimental.pallas import tpu as pltpu
from jax.sharding import PartitionSpec as P

NZ, NH, NL, NX, NU = 8, 2, 4, 4, 2
NY = NH * NL
ROWS = 128
HALF = ROWS // 2
SUBAP = 2048
SHARDS = NY * NX * NU
PIECES = NZ
TILE = NU * ROWS
TILES = SHARDS // NU
TILES_SENSOR = SUBAP // TILE
SLOTS = 16
CHUNK = 4
AHEAD = 3
MESH = pl.DeviceIdType.MESH
damping = 0.4
f32, bf16 = jnp.float32, jnp.bfloat16


def kernel(
    telemetry_in, scales_in, bands_in, noise_in, start, target, out1, out2,
    telemetry, scales, bands, noise, loaded, joined, colb, rowp, srow, inv, cov, dist, acc, bsend, brecv, dsend, drecv,
    tgt, noises, noi, low1, low2, cbuf, zbuf1, zbuf2, ebuf1, ebuf2,
    send_a, recv_a, send_r, recv_r, send_t, recv_t, send_n, recv_n, send_b, recv_b,
    send_c, recv_c, send_d, recv_d, send_g, recv_g, send_h, recv_h, send_e, recv_e, send_f, recv_f,
):
    row, col = lax.axis_index("row"), lax.axis_index("col")
    z, h = col // NH, col % NH
    l, x, u = row // (NX * NU), row // NU % NX, row % NU
    y = h * NL + l

    def rowid(yy, xx, uu):
        return yy % NL * (NX * NU) + xx * NU + uu

    def colid(zz, yy):
        return zz * NH + yy // NL

    def at(zz, yy, xx, uu):
        return rowid(yy, xx, uu), colid(zz, yy)

    def shard(yy, xx, uu):
        return (yy * NX + xx) * NU + uu

    def remote(src, dst, ssem, rsem, dev):
        return pltpu.make_async_remote_copy(
            src_ref=src, dst_ref=dst, send_sem=ssem, recv_sem=rsem, device_id=dev, device_id_type=MESH
        )

    def put_maybe_self(src, dst, ssem, rsem, dev):
        mine = (dev[0] == row) & (dev[1] == col)

        @pl.when(mine)
        def _():
            pltpu.make_async_copy(src, dst, rsem).start()

        @pl.when(jnp.logical_not(mine))
        def _():
            remote(src, dst, ssem, rsem, dev).start()

    me = shard(y, x, u)
    here = (row, col)
    xl, xr, xo = (x + NX - 1) % NX, (x + 1) % NX, (x + 2) % NX

    def near(i, start, size):
        return (start + i % 2 * ((i + 1) // 2) - (1 - i % 2) * (i // 2) + size) % size

    def y_of(i):
        return near(i, y, NY)

    def piece(i):
        return near(PIECES - 1 - i, z, NZ)

    zs = [near(i, z, NZ) for i in range(NZ - 1, 0, -1)]

    barrier = pltpu.get_barrier_semaphore()
    greet = [at(zz, y, x, u) for zz in zs] + [at(z, y_of(i), x, u) for i in range(1, NY)]
    greet += [at(z, y, xl, u), at(z, y, xr, u), at(z, y, xo, u), at(z, y, x, 1 - u)]
    for dev in greet:
        pl.semaphore_signal(barrier, inc=1, device_id=dev, device_id_type=MESH)

    loads = [
        pltpu.make_async_copy(src, dst, loaded.at[k])
        for k, (src, dst) in enumerate(
            (
                (telemetry_in, telemetry),
                (scales_in, scales),
                (start, joined.at[pl.ds(HALF, HALF)]),
                (bands_in, bands),
                (noise_in, noise),
            )
        )
    ]
    for load in loads:
        load.start()

    p0 = (l % 2 * (NX * NU) + x * NU + u) * ROWS
    base_d = (
        p0 + lax.broadcasted_iota(jnp.int32, (ROWS, TILE), 0) - lax.broadcasted_iota(jnp.int32, (ROWS, TILE), 1)
    )
    for t in range(TILES_SENSOR):
        dist[t] = jnp.abs(base_d - t * TILE).astype(f32)
    acc[...] = jnp.zeros_like(acc)
    for load in loads:
        load.wait()

    slopes = telemetry[...].astype(f32) * scales[...].astype(f32) * (1.0 / 128.0)
    joined[:HALF, :] = slopes.astype(bf16)
    for s in range(SLOTS):
        noises[s] = jnp.broadcast_to(noise[s : s + 1, :], (8, ROWS))
    colb[me] = joined[...]
    rowp[z] = joined[:HALF, :]

    for i in range(PIECES):
        for k in range(NL):
            a, b = NL * piece(i) + y // 2, NL * z + k
            band = bands[jnp.minimum(a, b), jnp.maximum(a, b)].astype(f32)
            inv[i * NL + k] = 1.0 / jnp.full((1, TILE), band, f32)
    pl.semaphore_wait(barrier, len(greet))

    other = at(z, y, x, 1 - u)
    across = [at(z, y, xo, u), at(z, y, xl, u), at(z, y, xr, u)]

    def plane_gather(src, buf, ssem, rsem):
        def send(k, s_src, s, dev):
            remote(s_src, buf.at[s], ssem.at[k], rsem.at[s], dev).start()

        def wait(s):
            remote(src, buf.at[s], ssem.at[0], rsem.at[s], here).wait_recv()

        def begin(beside):
            send(NY - 1 + len(across), src, me, other)
            for i in range(1, NY):
                send(i - 1, src, me, at(z, y_of(i), x, u))
                if i <= len(across):
                    send(NY - 2 + i, src, me, across[i - 1])
                beside(i)

        def y_step(i):
            s = shard(y_of(i), x, u)
            wait(s)
            for k, dev in enumerate((*across, other)):
                send(NY - 1 + NX * i + k, buf.at[s], s, dev)

        def x_step(i):
            for k, xx in enumerate((xl, xr, xo)):
                s = shard(y_of(i), xx, u)
                wait(s)
                send((1 + NX) * NY - 1 + (NX - 1) * i + k, buf.at[s], s, other)

        def other_step(i):
            for xx in range(NX):
                wait(shard(y_of(i), xx, 1 - u))

        def paced(step):
            def relay(i, carry):
                pl.when(i < NY)(lambda: x_step(i))

                @pl.when(i >= AHEAD)
                def _():
                    other_step(i - AHEAD)
                    step(i - AHEAD)

                return carry

            lax.fori_loop(0, NY + AHEAD, relay, 0)

        def drain():
            def one(k, carry):
                remote(src, buf.at[me], ssem.at[k], rsem.at[me], here).wait_send()
                return carry

            lax.fori_loop(0, 8 * NY - 1, one, 0)

        return begin, y_step, paced, drain

    mine_s = joined.at[pl.ds(0, HALF)]
    begin_a, y_step_a, paced_a, drain_a = plane_gather(joined, colb, send_a, recv_a)
    begin_a(lambda i: remote(mine_s, rowp.at[z], send_r.at[i], recv_r.at[z], at(near(i, z, NZ), y, x, u)).start())
    for i in range(1, NY):
        y_step_a(i)
    for zz in zs:
        remote(mine_s, rowp.at[zz], send_r.at[0], recv_r.at[zz], here).wait_recv()
    for i in range(PIECES):
        v = rowp[piece(i)].astype(f32) * (1.0 / 16384.0)
        srow[pl.ds(i * ROWS, ROWS), :] = jnp.transpose(v).astype(bf16)

    contract_last = (((1,), (1,)), ((), ()))
    slope_rows, panel_rows = slice(0, HALF), slice(HALF, ROWS)

    def wide(ref, t, part):
        return jnp.concatenate([ref[NU * t + i, part, :] for i in range(NX * NU)], axis=1)

    def rows_of(c):
        return pl.ds(c * CHUNK * ROWS, CHUNK * ROWS)

    def build(c, yy):
        span, t0 = rows_of(c), yy * NX
        entries = []
        for n in range(NX):
            cols = jnp.concatenate([colb[NU * (t0 + n) + i, slope_rows, :] for i in range(NU)], axis=1)
            raw = jnp.dot(srow[span, :], cols, preferred_element_type=f32)
            d = dist[yy % 2 * NX + n]
            parts = []
            for i in range(CHUNK):
                taper = jnp.maximum(0.0, 1.0 - d * inv[(c * CHUNK + i) * NL + yy // 2])
                parts.append((taper * raw[i * ROWS : (i + 1) * ROWS, :]).astype(bf16))
            entry = jnp.concatenate(parts, axis=0)
            cov[t0 + n, span, :] = entry
            entries.append(entry)
        acc[span, :] += lax.dot_general(
            jnp.concatenate(entries, axis=1), wide(colb, t0, panel_rows), contract_last, preferred_element_type=f32
        )

    def multiply(c, yy):
        span, t0 = rows_of(c), yy * NX
        entries = jnp.concatenate([cov[t0 + n, span, :] for n in range(NX)], axis=1)
        acc[span, :] += lax.dot_general(
            entries, wide(cbuf, t0, slice(None)), contract_last, preferred_element_type=f32
        )

    def send_rows(c, sbuf, rbuf, ssem, rsem):
        for i in range(c * CHUNK, (c + 1) * CHUNK):
            sbuf[i] = jnp.transpose(acc[pl.ds(i * ROWS, ROWS), :])
            if i < PIECES - 1:
                remote(sbuf.at[i], rbuf.at[z], ssem.at[i], rsem.at[z], at(piece(i), y, x, u)).start()

    def rest(step):
        def one(yy, carry):
            step(1, yy)
            return carry

        lax.fori_loop(0, NY, one, 0)

    paced_a(lambda i: build(0, y_of(i)))
    send_rows(0, bsend, brecv, send_b, recv_b)

    def target_part(slot):
        return target.at[:, pl.ds(pl.multiple_of(slot * ROWS, ROWS), ROWS)]

    source = (l == z // 2) & (x // 2 == z % 2)
    owner_dev = []
    for xx in range(NX):
        for uu in range(NU):
            slot = h * (NX * NU) + xx * NU + uu
            dev = ((2 * u + h) * (NX * NU) + xx * NU + uu, z * NH + x % NH)
            owner_dev.append((slot, dev))

    @pl.when(source)
    def _():
        for k, (slot, dev) in enumerate(owner_dev):
            put_maybe_self(target_part(slot), tgt, send_t.at[k], recv_t, dev)
            put_maybe_self(noises.at[slot], noi, send_n.at[k], recv_n, dev)

    rest(build)
    send_rows(1, bsend, brecv, send_b, recv_b)

    def collected(sbuf, rbuf, rsem):
        total = sbuf[PIECES - 1]
        for zz in zs:
            remote(sbuf.at[0], rbuf.at[zz], send_b.at[0], rsem.at[zz], here).wait_recv()
            total = total + rbuf[zz]
        return total

    remote(target_part(0), tgt, send_t.at[0], recv_t, here).wait_recv()
    remote(noises.at[0], noi, send_n.at[0], recv_n, here).wait_recv()
    s_own = joined[:HALF, :].astype(f32)
    x_own = joined[HALF:, :].astype(f32)
    raw_own = jnp.sum(s_own * s_own, axis=0, keepdims=True) * (1.0 / 16384.0)
    diag = raw_own + noi[0:1, :]
    weight = damping / diag
    extra = diag.astype(bf16).astype(f32) - raw_own.astype(bf16).astype(f32)
    tgt_own = tgt[...].astype(f32)

    first = x_own + weight * (tgt_own - (collected(bsend, brecv, recv_b) + extra * x_own))
    low1[...] = first.astype(bf16)

    slot_me = l % 2 * (NX * NU) + x * NU + u
    nearest = [near(i, z, NZ) for i in range(NZ)]

    def along_z(src, zbuf, ssem, rsem, i):
        remote(src, zbuf.at[z], ssem.at[i], rsem.at[z], at(near(i, z, NZ), y, x, u)).start()

    def along_z_sent(src, zbuf, ssem, rsem):
        for i in range(1, NZ):
            remote(src, zbuf.at[z], ssem.at[i], rsem.at[z], here).wait_send()

    def out_dev(zz, hh):
        return zz // 2 * (NX * NU) + (zz % 2 * 2 + h) * NU + l // 2, z * NH + hh

    def spread(src, zbuf, zsem, buf, ssem, rsem):
        for i, zz in enumerate(nearest):
            if i:
                remote(src, zbuf.at[zz], ssem.at[0], zsem.at[zz], here).wait_recv()
            for hh in range(NH):
                part = zbuf.at[zz] if i else src
                put_maybe_self(part, buf.at[slot_me], ssem.at[i * NH + hh], rsem.at[slot_me], out_dev(zz, hh))

    def spread_sent(src, buf, ssem, rsem):
        for i, zz in enumerate(nearest):
            for hh in range(NH):
                dev = out_dev(zz, hh)

                @pl.when(jnp.logical_not((dev[0] == row) & (dev[1] == col)))
                def _():
                    remote(src, buf.at[slot_me], ssem.at[i * NH + hh], rsem.at[slot_me], dev).wait_send()

    def unpack_out(src, buf, rsem, out):
        for s in range(SLOTS):
            remote(src, buf.at[s], send_e.at[0], rsem.at[s], here).wait_recv()
            out[:, pl.ds(s * ROWS, ROWS)] = buf[s]

    begin_c, y_step_c, paced_c, drain_c = plane_gather(low1, cbuf, send_c, recv_c)
    begin_c(lambda i: along_z(low1, zbuf1, send_g, recv_g, i))
    cbuf[me] = low1[...]
    acc[...] = jnp.zeros_like(acc)
    for i in range(1, NY):
        y_step_c(i)
    paced_c(lambda i: multiply(0, y_of(i)))
    send_rows(0, dsend, drecv, send_d, recv_d)
    spread(low1, zbuf1, recv_g, ebuf1, send_e, recv_e)
    rest(multiply)
    send_rows(1, dsend, drecv, send_d, recv_d)

    product1 = collected(dsend, drecv, recv_d) + extra * first.astype(bf16).astype(f32)
    low2[...] = (first + weight * (tgt_own - product1)).astype(bf16)
    for i in range(1, NZ):
        along_z(low2, zbuf2, send_h, recv_h, i)
    spread(low2, zbuf2, recv_h, ebuf2, send_f, recv_f)
    unpack_out(low1, ebuf1, recv_e, out1)
    unpack_out(low2, ebuf2, recv_f, out2)

    drain_a()
    drain_c()
    for i in range(1, NZ):
        remote(mine_s, rowp.at[z], send_r.at[i], recv_r.at[z], here).wait_send()

    @pl.when(source)
    def _():
        for k, (slot, dev) in enumerate(owner_dev):
            @pl.when(jnp.logical_not((dev[0] == row) & (dev[1] == col)))
            def _():
                remote(target_part(slot), tgt, send_t.at[k], recv_t, dev).wait_send()
                remote(noises.at[slot], noi, send_n.at[k], recv_n, dev).wait_send()

    for i in range(PIECES - 1):
        remote(bsend.at[i], brecv.at[z], send_b.at[i], recv_b.at[z], here).wait_send()
        remote(dsend.at[i], drecv.at[z], send_d.at[i], recv_d.at[z], here).wait_send()

    along_z_sent(low1, zbuf1, send_g, recv_g)
    along_z_sent(low2, zbuf2, send_h, recv_h)
    spread_sent(low1, ebuf1, send_e, recv_e)
    spread_sent(low2, ebuf2, send_f, recv_f)


def on_device(telemetry, scales, bands, noise, start, target):
    vmem = pl.BlockSpec(memory_space=pltpu.VMEM)
    dma, gathers = pltpu.SemaphoreType.DMA, SHARDS
    out = jax.ShapeDtypeStruct(target.shape[::-1], bf16)
    part = (HALF, ROWS)
    first, second = pl.pallas_call(
        kernel,
        out_shape=(out, out),
        in_specs=[pl.BlockSpec(memory_space=pltpu.HBM)] * 6,
        out_specs=(vmem, vmem),
        scratch_shapes=[
            pltpu.VMEM(part, jnp.int32),
            pltpu.VMEM((1, ROWS), jnp.int32),
            pltpu.SMEM(bands.shape, jnp.int32),
            pltpu.VMEM((SLOTS, ROWS), f32),
            dma((5,)),
            pltpu.VMEM((ROWS, ROWS), bf16),
            pltpu.VMEM((SHARDS, ROWS, ROWS), bf16),
            pltpu.VMEM((PIECES, *part), bf16),
            pltpu.VMEM((PIECES * ROWS, HALF), bf16),
            pltpu.VMEM((PIECES * NL, 1, TILE), f32),
            pltpu.VMEM((TILES, PIECES * ROWS, TILE), bf16),
            pltpu.VMEM((TILES_SENSOR, ROWS, TILE), f32),
            pltpu.VMEM((PIECES * ROWS, HALF), f32),
            pltpu.VMEM((PIECES, *part), f32),
            pltpu.VMEM((PIECES, *part), f32),
            pltpu.VMEM((PIECES, *part), f32),
            pltpu.VMEM((PIECES, *part), f32),
            pltpu.VMEM(part, bf16),
            pltpu.VMEM((SLOTS, 8, ROWS), f32),
            pltpu.VMEM((8, ROWS), f32),
            pltpu.VMEM(part, bf16),
            pltpu.VMEM(part, bf16),
            pltpu.VMEM((SHARDS, *part), bf16),
            pltpu.VMEM((NZ, *part), bf16),
            pltpu.VMEM((NZ, *part), bf16),
            pltpu.VMEM((SLOTS, *part), bf16),
            pltpu.VMEM((SLOTS, *part), bf16),
            dma((gathers,)), dma((SHARDS,)),
            dma((NZ,)), dma((NZ,)),
            dma((8,)), dma,
            dma((8,)), dma,
            dma((NZ,)), dma((NZ,)),
            dma((gathers,)), dma((SHARDS,)),
            dma((NZ,)), dma((NZ,)),
            dma((NZ,)), dma((NZ,)),
            dma((NZ,)), dma((NZ,)),
            dma((SLOTS,)), dma((SLOTS,)),
            dma((SLOTS,)), dma((SLOTS,)),
        ],
        compiler_params=pltpu.CompilerParams(
            collective_id=0, has_side_effects=True, vmem_limit_bytes=40 * 2**20
        ),
    )(*[pltpu.with_memory_space_constraint(a, pltpu.HBM) for a in (
        telemetry.T, scales.reshape(1, ROWS), bands, noise.reshape(SLOTS, ROWS), start.T, target.T
    )])
    return first.T.astype(f32), second.T.astype(f32)


def solution(mesh):
    placed = (P(("col", "row"), None), P(("col", "row")), P(), P("row"), P(("col", "row"), None), P("row", None))
    return jax.shard_map(
        on_device,
        mesh=mesh,
        in_specs=placed,
        out_specs=(P("row", None), P("row", None)),
        check_vma=False,
    )
```

```python
import jax
import jax.numpy as jnp
from jax import lax
from jax.experimental import pallas as pl
from jax.experimental.pallas import tpu as pltpu
from jax.sharding import PartitionSpec as P

NZ, NH, NL, NX, NU = 8, 2, 4, 4, 2
NY = NH * NL
ROWS = 128
HALF = ROWS // 2
SUBAP = 2048
SHARDS = NY * NX * NU
PIECES = NZ
TILE = NU * ROWS
TILES = SHARDS // NU
TILES_SENSOR = SUBAP // TILE
SLOTS = 16
CHUNK = 4
AHEAD = 2
MESH = pl.DeviceIdType.MESH
damping = 0.4
f32, bf16 = jnp.float32, jnp.bfloat16


def kernel(
    telemetry_in, scales_in, bands_in, noise_in, start, target, out1, out2,
    telemetry, scales, bands, noise, loaded, joined, colb, rowp, srow, inv, cov, dist, acc, bsend, brecv, dsend, drecv,
    tgt, noises, noi, low1, low2, cbuf, zbuf1, zbuf2, ebuf1, ebuf2,
    send_a, recv_a, send_r, recv_r, send_t, recv_t, send_n, recv_n, send_b, recv_b,
    send_c, recv_c, send_d, recv_d, send_g, recv_g, send_h, recv_h, send_e, recv_e, send_f, recv_f,
):
    row, col = lax.axis_index("row"), lax.axis_index("col")
    z, h = col // NH, col % NH
    l, x, u = row // (NX * NU), row // NU % NX, row % NU
    y = h * NL + l

    def rowid(yy, xx, uu):
        return yy % NL * (NX * NU) + xx * NU + uu

    def colid(zz, yy):
        return zz * NH + yy // NL

    def at(zz, yy, xx, uu):
        return rowid(yy, xx, uu), colid(zz, yy)

    def shard(yy, xx, uu):
        return (yy * NX + xx) * NU + uu

    def remote(src, dst, ssem, rsem, dev):
        return pltpu.make_async_remote_copy(
            src_ref=src, dst_ref=dst, send_sem=ssem, recv_sem=rsem, device_id=dev, device_id_type=MESH
        )

    def put_maybe_self(src, dst, ssem, rsem, dev):
        mine = (dev[0] == row) & (dev[1] == col)

        @pl.when(mine)
        def _():
            pltpu.make_async_copy(src, dst, rsem).start()

        @pl.when(jnp.logical_not(mine))
        def _():
            remote(src, dst, ssem, rsem, dev).start()

    me = shard(y, x, u)
    here = (row, col)
    xl, xr, xo = (x + NX - 1) % NX, (x + 1) % NX, (x + 2) % NX

    def near(i, start, size):
        return (start + i % 2 * ((i + 1) // 2) - (1 - i % 2) * (i // 2) + size) % size

    def y_of(i):
        return near(i, y, NY)

    def piece(i):
        return near(PIECES - 1 - i, z, NZ)

    zs = [near(i, z, NZ) for i in range(NZ - 1, 0, -1)]

    barrier = pltpu.get_barrier_semaphore()
    greet = [at(zz, y, x, u) for zz in zs] + [at(z, y_of(i), x, u) for i in range(1, NY)]
    greet += [at(z, y, xl, u), at(z, y, xr, u), at(z, y, xo, u), at(z, y, x, 1 - u)]
    for dev in greet:
        pl.semaphore_signal(barrier, inc=1, device_id=dev, device_id_type=MESH)

    loads = [
        pltpu.make_async_copy(src, dst, loaded.at[k])
        for k, (src, dst) in enumerate(
            (
                (telemetry_in, telemetry),
                (scales_in, scales),
                (start, joined.at[pl.ds(HALF, HALF)]),
                (bands_in, bands),
                (noise_in, noise),
            )
        )
    ]
    for load in loads:
        load.start()

    p0 = (l % 2 * (NX * NU) + x * NU + u) * ROWS
    base_d = (
        p0 + lax.broadcasted_iota(jnp.int32, (ROWS, TILE), 0) - lax.broadcasted_iota(jnp.int32, (ROWS, TILE), 1)
    )
    for t in range(TILES_SENSOR):
        dist[t] = jnp.abs(base_d - t * TILE).astype(f32)
    acc[...] = jnp.zeros_like(acc)
    for load in loads:
        load.wait()

    slopes = telemetry[...].astype(f32) * scales[...].astype(f32) * (1.0 / 128.0)
    joined[:HALF, :] = slopes.astype(bf16)
    for s in range(SLOTS):
        noises[s] = jnp.broadcast_to(noise[s : s + 1, :], (8, ROWS))
    colb[me] = joined[...]
    rowp[z] = joined[:HALF, :]

    for i in range(PIECES):
        for k in range(NL):
            a, b = NL * piece(i) + y // 2, NL * z + k
            band = bands[jnp.minimum(a, b), jnp.maximum(a, b)].astype(f32)
            inv[i * NL + k] = 1.0 / jnp.full((1, TILE), band, f32)
    pl.semaphore_wait(barrier, len(greet))

    other = at(z, y, x, 1 - u)
    across = [at(z, y, xo, u), at(z, y, xl, u), at(z, y, xr, u)]

    def plane_gather(src, buf, ssem, rsem):
        def send(k, s_src, s, dev):
            remote(s_src, buf.at[s], ssem.at[k], rsem.at[s], dev).start()

        def wait(s):
            remote(src, buf.at[s], ssem.at[0], rsem.at[s], here).wait_recv()

        def begin(beside):
            send(NY - 1 + len(across), src, me, other)
            for i in range(1, NY):
                send(i - 1, src, me, at(z, y_of(i), x, u))
                if i <= len(across):
                    send(NY - 2 + i, src, me, across[i - 1])
                beside(i)

        def y_step(i):
            s = shard(y_of(i), x, u)
            wait(s)
            for k, dev in enumerate((*across, other)):
                send(NY - 1 + NX * i + k, buf.at[s], s, dev)

        def x_step(i):
            for k, xx in enumerate((xl, xr, xo)):
                s = shard(y_of(i), xx, u)
                wait(s)
                send((1 + NX) * NY - 1 + (NX - 1) * i + k, buf.at[s], s, other)

        def other_step(i):
            for xx in range(NX):
                wait(shard(y_of(i), xx, 1 - u))

        def paced(step):
            def relay(i, carry):
                pl.when(i < NY)(lambda: x_step(i))

                other_step(i - AHEAD)
                step(i - AHEAD)
                return carry

            lax.fori_loop(AHEAD, NY + AHEAD, relay, 0)

        def drain():
            def one(k, carry):
                remote(src, buf.at[me], ssem.at[k], rsem.at[me], here).wait_send()
                return carry

            lax.fori_loop(0, 8 * NY - 1, one, 0)

        def ahead():
            for i in range(1, NY - 1):
                y_step(i)
            x_step(0)
            y_step(NY - 1)
            for i in range(1, AHEAD):
                x_step(i)

        return begin, ahead, paced, drain

    mine_s = joined.at[pl.ds(0, HALF)]
    begin_a, ahead_a, paced_a, drain_a = plane_gather(joined, colb, send_a, recv_a)
    begin_a(lambda i: remote(mine_s, rowp.at[z], send_r.at[i], recv_r.at[z], at(near(i, z, NZ), y, x, u)).start())
    ahead_a()
    for zz in zs:
        remote(mine_s, rowp.at[zz], send_r.at[0], recv_r.at[zz], here).wait_recv()
    for i in range(PIECES):
        v = rowp[piece(i)].astype(f32) * (1.0 / 16384.0)
        srow[pl.ds(i * ROWS, ROWS), :] = jnp.transpose(v).astype(bf16)

    contract_last = (((1,), (1,)), ((), ()))
    slope_rows, panel_rows = slice(0, HALF), slice(HALF, ROWS)

    def wide(ref, t, part):
        return jnp.concatenate([ref[NU * t + i, part, :] for i in range(NX * NU)], axis=1)

    def rows_of(c):
        return pl.ds(c * CHUNK * ROWS, CHUNK * ROWS)

    def build(c, yy):
        span, t0 = rows_of(c), yy * NX
        entries = []
        for n in range(NX):
            cols = jnp.concatenate([colb[NU * (t0 + n) + i, slope_rows, :] for i in range(NU)], axis=1)
            raw = jnp.dot(srow[span, :], cols, preferred_element_type=f32)
            d = dist[yy % 2 * NX + n]
            parts = []
            for i in range(CHUNK):
                taper = jnp.maximum(0.0, 1.0 - d * inv[(c * CHUNK + i) * NL + yy // 2])
                parts.append((taper * raw[i * ROWS : (i + 1) * ROWS, :]).astype(bf16))
            entry = jnp.concatenate(parts, axis=0)
            cov[t0 + n, span, :] = entry
            entries.append(entry)
        acc[span, :] += lax.dot_general(
            jnp.concatenate(entries, axis=1), wide(colb, t0, panel_rows), contract_last, preferred_element_type=f32
        )

    def multiply(c, yy):
        span, t0 = rows_of(c), yy * NX
        entries = jnp.concatenate([cov[t0 + n, span, :] for n in range(NX)], axis=1)
        acc[span, :] += lax.dot_general(
            entries, wide(cbuf, t0, slice(None)), contract_last, preferred_element_type=f32
        )

    def send_rows(c, sbuf, rbuf, ssem, rsem):
        for i in range(c * CHUNK, (c + 1) * CHUNK):
            sbuf[i] = jnp.transpose(acc[pl.ds(i * ROWS, ROWS), :])
            if i < PIECES - 1:
                remote(sbuf.at[i], rbuf.at[z], ssem.at[i], rsem.at[z], at(piece(i), y, x, u)).start()

    def rest(step):
        def one(yy, carry):
            step(1, yy)
            return carry

        lax.fori_loop(0, NY, one, 0)

    paced_a(lambda i: build(0, y_of(i)))
    send_rows(0, bsend, brecv, send_b, recv_b)

    def target_part(slot):
        return target.at[:, pl.ds(pl.multiple_of(slot * ROWS, ROWS), ROWS)]

    source = (l == z // 2) & (x // 2 == z % 2)
    owner_dev = []
    for xx in range(NX):
        for uu in range(NU):
            slot = h * (NX * NU) + xx * NU + uu
            dev = ((2 * u + h) * (NX * NU) + xx * NU + uu, z * NH + x % NH)
            owner_dev.append((slot, dev))

    @pl.when(source)
    def _():
        for k, (slot, dev) in enumerate(owner_dev):
            put_maybe_self(target_part(slot), tgt, send_t.at[k], recv_t, dev)
            put_maybe_self(noises.at[slot], noi, send_n.at[k], recv_n, dev)

    rest(build)
    send_rows(1, bsend, brecv, send_b, recv_b)

    def collected(sbuf, rbuf, rsem):
        total = sbuf[PIECES - 1]
        for zz in zs:
            remote(sbuf.at[0], rbuf.at[zz], send_b.at[0], rsem.at[zz], here).wait_recv()
            total = total + rbuf[zz]
        return total

    remote(target_part(0), tgt, send_t.at[0], recv_t, here).wait_recv()
    remote(noises.at[0], noi, send_n.at[0], recv_n, here).wait_recv()
    s_own = joined[:HALF, :].astype(f32)
    x_own = joined[HALF:, :].astype(f32)
    raw_own = jnp.sum(s_own * s_own, axis=0, keepdims=True) * (1.0 / 16384.0)
    diag = raw_own + noi[0:1, :]
    weight = damping / diag
    extra = diag.astype(bf16).astype(f32) - raw_own.astype(bf16).astype(f32)
    tgt_own = tgt[...].astype(f32)

    first = x_own + weight * (tgt_own - (collected(bsend, brecv, recv_b) + extra * x_own))
    low1[...] = first.astype(bf16)

    slot_me = l % 2 * (NX * NU) + x * NU + u
    nearest = [near(i, z, NZ) for i in range(NZ)]

    def along_z(src, zbuf, ssem, rsem, i):
        remote(src, zbuf.at[z], ssem.at[i], rsem.at[z], at(near(i, z, NZ), y, x, u)).start()

    def along_z_sent(src, zbuf, ssem, rsem):
        for i in range(1, NZ):
            remote(src, zbuf.at[z], ssem.at[i], rsem.at[z], here).wait_send()

    def out_dev(zz, hh):
        return zz // 2 * (NX * NU) + (zz % 2 * 2 + h) * NU + l // 2, z * NH + hh

    def spread(src, zbuf, zsem, buf, ssem, rsem):
        for i, zz in enumerate(nearest):
            if i:
                remote(src, zbuf.at[zz], ssem.at[0], zsem.at[zz], here).wait_recv()
            for hh in range(NH):
                part = zbuf.at[zz] if i else src
                put_maybe_self(part, buf.at[slot_me], ssem.at[i * NH + hh], rsem.at[slot_me], out_dev(zz, hh))

    def spread_sent(src, buf, ssem, rsem):
        for i, zz in enumerate(nearest):
            for hh in range(NH):
                dev = out_dev(zz, hh)

                @pl.when(jnp.logical_not((dev[0] == row) & (dev[1] == col)))
                def _():
                    remote(src, buf.at[slot_me], ssem.at[i * NH + hh], rsem.at[slot_me], dev).wait_send()

    def unpack_out(src, buf, rsem, out):
        for s in range(SLOTS):
            remote(src, buf.at[s], send_e.at[0], rsem.at[s], here).wait_recv()
            out[:, pl.ds(s * ROWS, ROWS)] = buf[s]

    begin_c, ahead_c, paced_c, drain_c = plane_gather(low1, cbuf, send_c, recv_c)
    begin_c(lambda i: along_z(low1, zbuf1, send_g, recv_g, i))
    cbuf[me] = low1[...]
    acc[...] = jnp.zeros_like(acc)
    ahead_c()
    paced_c(lambda i: multiply(0, y_of(i)))
    send_rows(0, dsend, drecv, send_d, recv_d)
    spread(low1, zbuf1, recv_g, ebuf1, send_e, recv_e)
    rest(multiply)
    send_rows(1, dsend, drecv, send_d, recv_d)

    product1 = collected(dsend, drecv, recv_d) + extra * first.astype(bf16).astype(f32)
    low2[...] = (first + weight * (tgt_own - product1)).astype(bf16)
    for i in range(1, NZ):
        along_z(low2, zbuf2, send_h, recv_h, i)
    spread(low2, zbuf2, recv_h, ebuf2, send_f, recv_f)
    unpack_out(low1, ebuf1, recv_e, out1)
    unpack_out(low2, ebuf2, recv_f, out2)

    drain_a()
    drain_c()
    for i in range(1, NZ):
        remote(mine_s, rowp.at[z], send_r.at[i], recv_r.at[z], here).wait_send()

    @pl.when(source)
    def _():
        for k, (slot, dev) in enumerate(owner_dev):
            @pl.when(jnp.logical_not((dev[0] == row) & (dev[1] == col)))
            def _():
                remote(target_part(slot), tgt, send_t.at[k], recv_t, dev).wait_send()
                remote(noises.at[slot], noi, send_n.at[k], recv_n, dev).wait_send()

    for i in range(PIECES - 1):
        remote(bsend.at[i], brecv.at[z], send_b.at[i], recv_b.at[z], here).wait_send()
        remote(dsend.at[i], drecv.at[z], send_d.at[i], recv_d.at[z], here).wait_send()

    along_z_sent(low1, zbuf1, send_g, recv_g)
    along_z_sent(low2, zbuf2, send_h, recv_h)
    spread_sent(low1, ebuf1, send_e, recv_e)
    spread_sent(low2, ebuf2, send_f, recv_f)


def on_device(telemetry, scales, bands, noise, start, target):
    vmem = pl.BlockSpec(memory_space=pltpu.VMEM)
    dma, gathers = pltpu.SemaphoreType.DMA, SHARDS
    out = jax.ShapeDtypeStruct(target.shape[::-1], bf16)
    part = (HALF, ROWS)
    first, second = pl.pallas_call(
        kernel,
        out_shape=(out, out),
        in_specs=[pl.BlockSpec(memory_space=pltpu.HBM)] * 6,
        out_specs=(vmem, vmem),
        scratch_shapes=[
            pltpu.VMEM(part, jnp.int32),
            pltpu.VMEM((1, ROWS), jnp.int32),
            pltpu.SMEM(bands.shape, jnp.int32),
            pltpu.VMEM((SLOTS, ROWS), f32),
            dma((5,)),
            pltpu.VMEM((ROWS, ROWS), bf16),
            pltpu.VMEM((SHARDS, ROWS, ROWS), bf16),
            pltpu.VMEM((PIECES, *part), bf16),
            pltpu.VMEM((PIECES * ROWS, HALF), bf16),
            pltpu.VMEM((PIECES * NL, 1, TILE), f32),
            pltpu.VMEM((TILES, PIECES * ROWS, TILE), bf16),
            pltpu.VMEM((TILES_SENSOR, ROWS, TILE), f32),
            pltpu.VMEM((PIECES * ROWS, HALF), f32),
            pltpu.VMEM((PIECES, *part), f32),
            pltpu.VMEM((PIECES, *part), f32),
            pltpu.VMEM((PIECES, *part), f32),
            pltpu.VMEM((PIECES, *part), f32),
            pltpu.VMEM(part, bf16),
            pltpu.VMEM((SLOTS, 8, ROWS), f32),
            pltpu.VMEM((8, ROWS), f32),
            pltpu.VMEM(part, bf16),
            pltpu.VMEM(part, bf16),
            pltpu.VMEM((SHARDS, *part), bf16),
            pltpu.VMEM((NZ, *part), bf16),
            pltpu.VMEM((NZ, *part), bf16),
            pltpu.VMEM((SLOTS, *part), bf16),
            pltpu.VMEM((SLOTS, *part), bf16),
            dma((gathers,)), dma((SHARDS,)),
            dma((NZ,)), dma((NZ,)),
            dma((8,)), dma,
            dma((8,)), dma,
            dma((NZ,)), dma((NZ,)),
            dma((gathers,)), dma((SHARDS,)),
            dma((NZ,)), dma((NZ,)),
            dma((NZ,)), dma((NZ,)),
            dma((NZ,)), dma((NZ,)),
            dma((SLOTS,)), dma((SLOTS,)),
            dma((SLOTS,)), dma((SLOTS,)),
        ],
        compiler_params=pltpu.CompilerParams(
            collective_id=0, has_side_effects=True, vmem_limit_bytes=40 * 2**20
        ),
    )(*[pltpu.with_memory_space_constraint(a, pltpu.HBM) for a in (
        telemetry.T, scales.reshape(1, ROWS), bands, noise.reshape(SLOTS, ROWS), start.T, target.T
    )])
    return first.T.astype(f32), second.T.astype(f32)


def solution(mesh):
    placed = (P(("col", "row"), None), P(("col", "row")), P(), P("row"), P(("col", "row"), None), P("row", None))
    return jax.shard_map(
        on_device,
        mesh=mesh,
        in_specs=placed,
        out_specs=(P("row", None), P("row", None)),
        check_vma=False,
    )
```

```python
import jax
import jax.numpy as jnp
from jax import lax
from jax.experimental import pallas as pl
from jax.experimental.pallas import tpu as pltpu
from jax.sharding import PartitionSpec as P

NZ, NH, NL, NX, NU = 8, 2, 4, 4, 2
NY = NH * NL
ROWS = 128
HALF = ROWS // 2
SUBAP = 2048
SHARDS = NY * NX * NU
PIECES = NZ
TILE = NU * ROWS
TILES = SHARDS // NU
TILES_SENSOR = SUBAP // TILE
SLOTS = 16
CHUNK = 4
AHEAD = 2
MESH = pl.DeviceIdType.MESH
damping = 0.4
f32, bf16 = jnp.float32, jnp.bfloat16


def kernel(
    telemetry_in, scales_in, bands_in, noise_in, start, target, out1, out2,
    telemetry, scales, bands, noise, loaded, joined, colb, rowp, srow, inv, cov, dist, acc, bsend, brecv, dsend, drecv,
    tgt, noises, noi, low1, low2, cbuf, zbuf1, zbuf2, ebuf1, ebuf2,
    send_a, recv_a, send_r, recv_r, send_t, recv_t, send_n, recv_n, send_b, recv_b,
    send_c, recv_c, send_d, recv_d, send_g, recv_g, send_h, recv_h, send_e, recv_e, send_f, recv_f,
):
    row, col = lax.axis_index("row"), lax.axis_index("col")
    z, h = col // NH, col % NH
    l, x, u = row // (NX * NU), row // NU % NX, row % NU
    y = h * NL + l

    def rowid(yy, xx, uu):
        return yy % NL * (NX * NU) + xx * NU + uu

    def colid(zz, yy):
        return zz * NH + yy // NL

    def at(zz, yy, xx, uu):
        return rowid(yy, xx, uu), colid(zz, yy)

    def shard(yy, xx, uu):
        return (yy * NX + xx) * NU + uu

    def remote(src, dst, ssem, rsem, dev):
        return pltpu.make_async_remote_copy(
            src_ref=src, dst_ref=dst, send_sem=ssem, recv_sem=rsem, device_id=dev, device_id_type=MESH
        )

    def put_maybe_self(src, dst, ssem, rsem, dev):
        mine = (dev[0] == row) & (dev[1] == col)

        @pl.when(mine)
        def _():
            pltpu.make_async_copy(src, dst, rsem).start()

        @pl.when(jnp.logical_not(mine))
        def _():
            remote(src, dst, ssem, rsem, dev).start()

    me = shard(y, x, u)
    here = (row, col)
    xl, xr, xo = (x + NX - 1) % NX, (x + 1) % NX, (x + 2) % NX

    def near(i, start, size):
        return (start + i % 2 * ((i + 1) // 2) - (1 - i % 2) * (i // 2) + size) % size

    def y_of(i):
        return near(i, y, NY)

    def piece(i):
        return near(PIECES - 1 - i, z, NZ)

    zs = [near(i, z, NZ) for i in range(NZ - 1, 0, -1)]

    barrier = pltpu.get_barrier_semaphore()
    greet = [at(zz, y, x, u) for zz in zs] + [at(z, y_of(i), x, u) for i in range(1, NY)]
    greet += [at(z, y, xl, u), at(z, y, xr, u), at(z, y, xo, u), at(z, y, x, 1 - u)]
    for dev in greet:
        pl.semaphore_signal(barrier, inc=1, device_id=dev, device_id_type=MESH)

    loads = [
        pltpu.make_async_copy(src, dst, loaded.at[k])
        for k, (src, dst) in enumerate(
            (
                (telemetry_in, telemetry),
                (scales_in, scales),
                (start, joined.at[pl.ds(HALF, HALF)]),
                (bands_in, bands),
                (noise_in, noise),
            )
        )
    ]
    for load in loads:
        load.start()

    p0 = (l % 2 * (NX * NU) + x * NU + u) * ROWS
    base_d = (
        p0 + lax.broadcasted_iota(jnp.int32, (ROWS, TILE), 0) - lax.broadcasted_iota(jnp.int32, (ROWS, TILE), 1)
    )
    for t in range(TILES_SENSOR):
        dist[t] = jnp.abs(base_d - t * TILE).astype(f32)
    acc[...] = jnp.zeros_like(acc)
    for load in loads:
        load.wait()

    slopes = telemetry[...].astype(f32) * scales[...].astype(f32) * (1.0 / 128.0)
    joined[:HALF, :] = slopes.astype(bf16)
    for s in range(SLOTS):
        noises[s] = jnp.broadcast_to(noise[s : s + 1, :], (8, ROWS))
    colb[me] = joined[...]
    rowp[z] = joined[:HALF, :]

    for i in range(PIECES):
        for k in range(NL):
            a, b = NL * piece(i) + y // 2, NL * z + k
            band = bands[jnp.minimum(a, b), jnp.maximum(a, b)].astype(f32)
            inv[i * NL + k] = 1.0 / jnp.full((1, TILE), band, f32)
    pl.semaphore_wait(barrier, len(greet))

    other = at(z, y, x, 1 - u)
    across = [at(z, y, xo, u), at(z, y, xl, u), at(z, y, xr, u)]

    def plane_gather(src, buf, ssem, rsem):
        def send(k, s_src, s, dev):
            remote(s_src, buf.at[s], ssem.at[k], rsem.at[s], dev).start()

        def wait(s):
            remote(src, buf.at[s], ssem.at[0], rsem.at[s], here).wait_recv()

        def begin(beside):
            send(NY - 1 + len(across), src, me, other)
            for i in range(1, NY):
                send(i - 1, src, me, at(z, y_of(i), x, u))
                if i <= len(across):
                    send(NY - 2 + i, src, me, across[i - 1])
                beside(i)

        def y_step(i):
            s = shard(y_of(i), x, u)
            wait(s)
            for k, dev in enumerate((*across, other)):
                send(NY - 1 + NX * i + k, buf.at[s], s, dev)

        def x_step(i):
            for k, xx in enumerate((xl, xr, xo)):
                s = shard(y_of(i), xx, u)
                wait(s)
                send((1 + NX) * NY - 1 + (NX - 1) * i + k, buf.at[s], s, other)

        def other_step(i):
            for xx in range(NX):
                wait(shard(y_of(i), xx, 1 - u))

        def paced(step):
            def relay(i, carry):
                pl.when(i < NY)(lambda: x_step(i))

                other_step(i - AHEAD)
                step(i - AHEAD)
                return carry

            lax.fori_loop(AHEAD, NY + AHEAD, relay, 0)

        def drain():
            def one(k, carry):
                remote(src, buf.at[me], ssem.at[k], rsem.at[me], here).wait_send()
                return carry

            lax.fori_loop(0, 8 * NY - 1, one, 0)

        def ahead():
            for i in range(1, NY - 1):
                y_step(i)
            x_step(0)
            y_step(NY - 1)
            for i in range(1, AHEAD):
                x_step(i)

        return begin, ahead, paced, drain

    mine_s = joined.at[pl.ds(0, HALF)]
    begin_a, ahead_a, paced_a, drain_a = plane_gather(joined, colb, send_a, recv_a)
    begin_a(lambda i: remote(mine_s, rowp.at[z], send_r.at[i], recv_r.at[z], at(near(i, z, NZ), y, x, u)).start())
    ahead_a()
    for zz in zs:
        remote(mine_s, rowp.at[zz], send_r.at[0], recv_r.at[zz], here).wait_recv()
    for i in range(PIECES):
        v = rowp[piece(i)].astype(f32) * (1.0 / 16384.0)
        srow[pl.ds(i * ROWS, ROWS), :] = jnp.transpose(v).astype(bf16)

    contract_last = (((1,), (1,)), ((), ()))
    slope_rows, panel_rows = slice(0, HALF), slice(HALF, ROWS)

    def wide(ref, t, part):
        return jnp.concatenate([ref[NU * t + i, part, :] for i in range(NX * NU)], axis=1)

    def rows_of(c):
        return pl.ds(c * CHUNK * ROWS, CHUNK * ROWS)

    def build(c, yy):
        span, t0 = rows_of(c), yy * NX
        entries = []
        for n in range(NX):
            cols = jnp.concatenate([colb[NU * (t0 + n) + i, slope_rows, :] for i in range(NU)], axis=1)
            raw = jnp.dot(srow[span, :], cols, preferred_element_type=f32)
            d = dist[yy % 2 * NX + n]
            parts = []
            for i in range(CHUNK):
                taper = jnp.maximum(0.0, 1.0 - d * inv[(c * CHUNK + i) * NL + yy // 2])
                parts.append((taper * raw[i * ROWS : (i + 1) * ROWS, :]).astype(bf16))
            entry = jnp.concatenate(parts, axis=0)
            cov[t0 + n, span, :] = entry
            entries.append(entry)
        acc[span, :] += lax.dot_general(
            jnp.concatenate(entries, axis=1), wide(colb, t0, panel_rows), contract_last, preferred_element_type=f32
        )

    def multiply(c, yy):
        span, t0 = rows_of(c), yy * NX
        entries = jnp.concatenate([cov[t0 + n, span, :] for n in range(NX)], axis=1)
        acc[span, :] += lax.dot_general(
            entries, wide(cbuf, t0, slice(None)), contract_last, preferred_element_type=f32
        )

    def send_rows(c, sbuf, rbuf, ssem, rsem):
        for i in range(c * CHUNK, (c + 1) * CHUNK):
            sbuf[i] = jnp.transpose(acc[pl.ds(i * ROWS, ROWS), :])
            if i < PIECES - 1:
                remote(sbuf.at[i], rbuf.at[z], ssem.at[i], rsem.at[z], at(piece(i), y, x, u)).start()

    def rest(step):
        def one(yy, carry):
            step(1, yy)
            return carry

        lax.fori_loop(0, NY, one, 0)

    paced_a(lambda i: build(0, y_of(i)))
    send_rows(0, bsend, brecv, send_b, recv_b)

    def target_part(slot):
        return target.at[:, pl.ds(pl.multiple_of(slot * ROWS, ROWS), ROWS)]

    source = (l == z // 2) & (x // 2 == z % 2)
    owner_dev = []
    for xx in range(NX):
        for uu in range(NU):
            slot = h * (NX * NU) + xx * NU + uu
            dev = ((2 * u + h) * (NX * NU) + xx * NU + uu, z * NH + x % NH)
            owner_dev.append((slot, dev))

    @pl.when(source)
    def _():
        for k, (slot, dev) in enumerate(owner_dev):
            put_maybe_self(target_part(slot), tgt, send_t.at[k], recv_t, dev)
            put_maybe_self(noises.at[slot], noi, send_n.at[k], recv_n, dev)

    rest(build)
    send_rows(1, bsend, brecv, send_b, recv_b)

    def collected(sbuf, rbuf, rsem):
        total = sbuf[PIECES - 1]
        for zz in zs:
            remote(sbuf.at[0], rbuf.at[zz], send_b.at[0], rsem.at[zz], here).wait_recv()
            total = total + rbuf[zz]
        return total

    remote(target_part(0), tgt, send_t.at[0], recv_t, here).wait_recv()
    remote(noises.at[0], noi, send_n.at[0], recv_n, here).wait_recv()
    s_own = joined[:HALF, :].astype(f32)
    x_own = joined[HALF:, :].astype(f32)
    raw_own = jnp.sum(s_own * s_own, axis=0, keepdims=True) * (1.0 / 16384.0)
    diag = raw_own + noi[0:1, :]
    weight = damping / diag
    extra = diag.astype(bf16).astype(f32) - raw_own.astype(bf16).astype(f32)
    tgt_own = tgt[...].astype(f32)

    first = x_own + weight * (tgt_own - (collected(bsend, brecv, recv_b) + extra * x_own))
    low1[...] = first.astype(bf16)

    slot_me = l % 2 * (NX * NU) + x * NU + u
    nearest = [near(i, z, NZ) for i in range(NZ)]

    def along_z(src, zbuf, ssem, rsem, i):
        remote(src, zbuf.at[z], ssem.at[i], rsem.at[z], at(near(i, z, NZ), y, x, u)).start()

    def along_z_sent(src, zbuf, ssem, rsem):
        for i in range(1, NZ):
            remote(src, zbuf.at[z], ssem.at[i], rsem.at[z], here).wait_send()

    def out_dev(zz, hh):
        return zz // 2 * (NX * NU) + (zz % 2 * 2 + h) * NU + l // 2, z * NH + hh

    def spread(src, zbuf, zsem, buf, ssem, rsem):
        for i, zz in enumerate(nearest):
            if i:
                remote(src, zbuf.at[zz], ssem.at[0], zsem.at[zz], here).wait_recv()
            for hh in range(NH):
                part = zbuf.at[zz] if i else src
                put_maybe_self(part, buf.at[slot_me], ssem.at[i * NH + hh], rsem.at[slot_me], out_dev(zz, hh))

    def spread_sent(src, buf, ssem, rsem):
        for i, zz in enumerate(nearest):
            for hh in range(NH):
                dev = out_dev(zz, hh)

                @pl.when(jnp.logical_not((dev[0] == row) & (dev[1] == col)))
                def _():
                    remote(src, buf.at[slot_me], ssem.at[i * NH + hh], rsem.at[slot_me], dev).wait_send()

    def unpack_out(src, buf, rsem, out):
        for s in range(SLOTS):
            remote(src, buf.at[s], send_e.at[0], rsem.at[s], here).wait_recv()
            out[:, pl.ds(s * ROWS, ROWS)] = buf[s]

    begin_c, ahead_c, paced_c, drain_c = plane_gather(low1, cbuf, send_c, recv_c)
    begin_c(lambda i: None)
    cbuf[me] = low1[...]
    acc[...] = jnp.zeros_like(acc)
    ahead_c()
    for i in range(1, NZ):
        along_z(low1, zbuf1, send_g, recv_g, i)
    paced_c(lambda i: multiply(0, y_of(i)))
    send_rows(0, dsend, drecv, send_d, recv_d)
    spread(low1, zbuf1, recv_g, ebuf1, send_e, recv_e)
    rest(multiply)
    send_rows(1, dsend, drecv, send_d, recv_d)

    product1 = collected(dsend, drecv, recv_d) + extra * first.astype(bf16).astype(f32)
    low2[...] = (first + weight * (tgt_own - product1)).astype(bf16)
    for i in range(1, NZ):
        along_z(low2, zbuf2, send_h, recv_h, i)
    spread(low2, zbuf2, recv_h, ebuf2, send_f, recv_f)
    unpack_out(low1, ebuf1, recv_e, out1)
    unpack_out(low2, ebuf2, recv_f, out2)

    drain_a()
    drain_c()
    for i in range(1, NZ):
        remote(mine_s, rowp.at[z], send_r.at[i], recv_r.at[z], here).wait_send()

    @pl.when(source)
    def _():
        for k, (slot, dev) in enumerate(owner_dev):
            @pl.when(jnp.logical_not((dev[0] == row) & (dev[1] == col)))
            def _():
                remote(target_part(slot), tgt, send_t.at[k], recv_t, dev).wait_send()
                remote(noises.at[slot], noi, send_n.at[k], recv_n, dev).wait_send()

    for i in range(PIECES - 1):
        remote(bsend.at[i], brecv.at[z], send_b.at[i], recv_b.at[z], here).wait_send()
        remote(dsend.at[i], drecv.at[z], send_d.at[i], recv_d.at[z], here).wait_send()

    along_z_sent(low1, zbuf1, send_g, recv_g)
    along_z_sent(low2, zbuf2, send_h, recv_h)
    spread_sent(low1, ebuf1, send_e, recv_e)
    spread_sent(low2, ebuf2, send_f, recv_f)


def on_device(telemetry, scales, bands, noise, start, target):
    vmem = pl.BlockSpec(memory_space=pltpu.VMEM)
    dma, gathers = pltpu.SemaphoreType.DMA, SHARDS
    out = jax.ShapeDtypeStruct(target.shape[::-1], bf16)
    part = (HALF, ROWS)
    first, second = pl.pallas_call(
        kernel,
        out_shape=(out, out),
        in_specs=[pl.BlockSpec(memory_space=pltpu.HBM)] * 6,
        out_specs=(vmem, vmem),
        scratch_shapes=[
            pltpu.VMEM(part, jnp.int32),
            pltpu.VMEM((1, ROWS), jnp.int32),
            pltpu.SMEM(bands.shape, jnp.int32),
            pltpu.VMEM((SLOTS, ROWS), f32),
            dma((5,)),
            pltpu.VMEM((ROWS, ROWS), bf16),
            pltpu.VMEM((SHARDS, ROWS, ROWS), bf16),
            pltpu.VMEM((PIECES, *part), bf16),
            pltpu.VMEM((PIECES * ROWS, HALF), bf16),
            pltpu.VMEM((PIECES * NL, 1, TILE), f32),
            pltpu.VMEM((TILES, PIECES * ROWS, TILE), bf16),
            pltpu.VMEM((TILES_SENSOR, ROWS, TILE), f32),
            pltpu.VMEM((PIECES * ROWS, HALF), f32),
            pltpu.VMEM((PIECES, *part), f32),
            pltpu.VMEM((PIECES, *part), f32),
            pltpu.VMEM((PIECES, *part), f32),
            pltpu.VMEM((PIECES, *part), f32),
            pltpu.VMEM(part, bf16),
            pltpu.VMEM((SLOTS, 8, ROWS), f32),
            pltpu.VMEM((8, ROWS), f32),
            pltpu.VMEM(part, bf16),
            pltpu.VMEM(part, bf16),
            pltpu.VMEM((SHARDS, *part), bf16),
            pltpu.VMEM((NZ, *part), bf16),
            pltpu.VMEM((NZ, *part), bf16),
            pltpu.VMEM((SLOTS, *part), bf16),
            pltpu.VMEM((SLOTS, *part), bf16),
            dma((gathers,)), dma((SHARDS,)),
            dma((NZ,)), dma((NZ,)),
            dma((8,)), dma,
            dma((8,)), dma,
            dma((NZ,)), dma((NZ,)),
            dma((gathers,)), dma((SHARDS,)),
            dma((NZ,)), dma((NZ,)),
            dma((NZ,)), dma((NZ,)),
            dma((NZ,)), dma((NZ,)),
            dma((SLOTS,)), dma((SLOTS,)),
            dma((SLOTS,)), dma((SLOTS,)),
        ],
        compiler_params=pltpu.CompilerParams(
            collective_id=0, has_side_effects=True, vmem_limit_bytes=40 * 2**20
        ),
    )(*[pltpu.with_memory_space_constraint(a, pltpu.HBM) for a in (
        telemetry.T, scales.reshape(1, ROWS), bands, noise.reshape(SLOTS, ROWS), start.T, target.T
    )])
    return first.T.astype(f32), second.T.astype(f32)


def solution(mesh):
    placed = (P(("col", "row"), None), P(("col", "row")), P(), P("row"), P(("col", "row"), None), P("row", None))
    return jax.shard_map(
        on_device,
        mesh=mesh,
        in_specs=placed,
        out_specs=(P("row", None), P("row", None)),
        check_vma=False,
    )
```
